32 devices in a mesh: groups: 2 (over y), gx: 16 (over z, x, core).
Axes of the slice: x: 2, y: 2, z: 4, core: 2. Of those that a mesh axis runs over, the one named last changes fastest.
Arguments:
- volume: bfloat16 [64, 16, 16, 512], P(None, 'gx', 'groups'), parts along dimension 2, may hold values from -6 to 6
- weights: bfloat16 [4, 4, 4, 64, 32], replicated, may hold values from -0.25 to 0.25
- cotangent: bfloat16 [32, 32, 32, 1024], P(None, 'gx', 'groups'), parts along dimension 2, may hold values from -6 to 6
Outputs:
- upsampled: bfloat16 [32, 32, 32, 1024], P(None, 'gx', 'groups'), parts along dimension 2
- volume_grad: bfloat16 [64, 16, 16, 512], P(None, 'gx', 'groups'), parts along dimension 2
- weight_grad: float32 [8, 4, 4, 64, 32], P('groups'), parts along dimension 0
The draws below stay inside these ranges and needn't reach their ends.
There are 2 independent parts, one for each index of `groups`. The reference program is written for one: setup_inputs(seed, part) draws one part's arguments, and reference() takes and returns one part's arrays. A program takes and returns all parts, laid end to end along the dimension named above; an argument that names none is the same for every part. Nothing has to cross between parts.
All inputs are finite; a program needn't handle non-finite values.
Results may differ from the reference program's by a relative error of at most 0.001.
Values may be sent and summed in bfloat16 or wider, within the bound.
No kernel may reach another device: no remote copies, remote signals or barrier semaphores. Data moves between devices by JAX's collectives and lax.ppermute only.
A program may use at most 128 MiB of HBM per device.

```python
import math
import jax
import jax.numpy as jnp
from jax import lax

CIN = 64
COUT = 32
NY = 8
NZ = 512
NX = 16


def shard_levels(key, dims, pieces, smallest, high):
    gain, own = 1.0, jax.random.fold_in(key, 6)
    for dim, shards_of in pieces:
        heights = jnp.exp(jax.random.uniform(jax.random.fold_in(own, dim), (shards_of,), jnp.float32, smallest / len(pieces), high / len(pieces)))
        gain = gain * jnp.repeat(heights, dims[dim] // shards_of).reshape([-1 if axis == dim else 1 for axis in range(len(dims))])
    return gain


def normal_values(stream_key, dims, deviation, most, cuts=(), kind=jnp.bfloat16):
    gain = shard_levels(stream_key, dims, cuts, -0.22, 0.18) if cuts else 1.0
    values = jax.random.normal(stream_key, dims, jnp.float32) * deviation * gain
    return jnp.minimum(jnp.maximum(values, -most), most).astype(kind)


def setup_inputs(seed: int = 0, part: int = 0) -> dict:
    keys = jax.random.split(jax.random.key(seed), 4)
    part_keys = jax.random.split(jax.random.fold_in(keys[3], part), 4)
    volume = normal_values(part_keys[0], (CIN, NX, NY, NZ), 1.0, 6.0, ((1, 16),))
    weights = normal_values(keys[1], (4, 4, 4, CIN, COUT), (8 * CIN) ** -0.5, 0.25)
    cotangent = normal_values(part_keys[2], (COUT, 2 * NX, 2 * NY, 2 * NZ), 1.0, 6.0, ((1, 16),))
    return dict(volume=volume, weights=weights, cotangent=cotangent)


def place_phases(getter, dimension):
    even_part = getter(1) + jnp.roll(getter(3), 1, dimension)
    odd_part = getter(2) + jnp.roll(getter(0), -1, dimension)
    paired = jnp.stack([even_part, odd_part], dimension + 1)
    new_shape = list(even_part.shape)
    new_shape[dimension] = new_shape[dimension] * 2
    return paired.reshape(new_shape)

def split_parity(source, dimension):
    new_shape = list(source.shape)
    new_shape[dimension:dimension + 1] = [new_shape[dimension] // 2, 2]
    paired = source.reshape(new_shape)
    return (lax.index_in_dim(paired, 0, dimension + 1, keepdims=False), lax.index_in_dim(paired, 1, dimension + 1, keepdims=False))

def select_taps(source, dimension):
    even_part, odd_part = split_parity(source, dimension)
    return [jnp.roll(odd_part, 1, dimension), even_part, odd_part, jnp.roll(even_part, -1, dimension)]

def reference(volume, weights, cotangent):
    highest = lax.Precision.HIGHEST
    volume_wide = volume.astype(jnp.float32)
    kernel = weights.astype(jnp.float32)

    def plane_term(tap_x):

        def row_term(tap_y):
            products = jnp.einsum('kcd,cxyz->kdxyz', kernel[tap_x, tap_y], volume_wide, precision=highest)
            return place_phases(lambda tap_z: products[tap_z], 3)
        return place_phases(row_term, 2)
    upsampled = place_phases(plane_term, 1).astype(jnp.bfloat16)
    volume_grad = jnp.zeros(volume.shape, jnp.float32)
    blocks = []
    for tap_x, x_piece in enumerate(select_taps(cotangent, 1)):
        row_blocks = []
        for tap_y, y_piece in enumerate(select_taps(x_piece, 2)):
            stacked = jnp.stack(select_taps(y_piece, 3), 0).astype(jnp.float32)
            volume_grad = volume_grad + jnp.einsum('kcd,kdxyz->cxyz', kernel[tap_x, tap_y], stacked, precision=highest)
            row_blocks.append(jnp.einsum('cxyz,kdxyz->kcd', volume_wide, stacked, precision=highest))
        blocks.append(jnp.stack(row_blocks, 0))
    weight_grad = (jnp.stack(blocks, 0) / math.sqrt(NX * NY * NZ)).astype(jnp.float32)
    return (upsampled, volume_grad.astype(jnp.bfloat16), weight_grad)
```

```python
import functools
import math

import jax
import jax.numpy as jnp
from jax import lax
from jax.experimental import pallas as pl
from jax.experimental.pallas import tpu as pltpu
from jax.sharding import PartitionSpec as P

F32 = jnp.float32
BF16 = jnp.bfloat16
NT = (((1,), (1,)), ((), ()))


def roles(core):
    inner = (1 - core, 2 - core, 3 * core)
    outer = (core, 1 + core, 3 - 3 * core)
    return inner, outer


def dot(a, b):
    return jnp.dot(a, b, preferred_element_type=F32)


def split_table():
    row = lax.broadcasted_iota(jnp.int32, (256, 256), 0)
    col = lax.broadcasted_iota(jnp.int32, (256, 256), 1)
    return (row == jnp.where(col < 128, 2 * col, 2 * col - 255)).astype(BF16)


def join_table():
    row = lax.broadcasted_iota(jnp.int32, (256, 256), 0)
    col = lax.broadcasted_iota(jnp.int32, (256, 256), 1)
    return (col == jnp.where(row < 128, 2 * row, 2 * row - 255)).astype(BF16)


def load_rows(ref, start, count, stride):
    return jnp.concatenate([ref[b, pl.ds(start, count, stride=stride), :] for b in range(ref.shape[0])], 1)


def store_rows(ref, start, stride, value):
    for b in range(ref.shape[0]):
        ref[b, pl.ds(start, value.shape[0], stride=stride), :] = value[:, 128 * b : 128 * b + 128]


def rows_by_y(source_ref, wide_ref, target_ref, ny):
    chans = source_ref.shape[0] // ny
    for b in range(wide_ref.shape[0]):
        wide_ref[b] = source_ref[:, 128 * b : 128 * b + 128].astype(F32)
    for y in range(ny):
        target_ref[y * chans : (y + 1) * chans, :] = load_rows(wide_ref, y, chans, ny).astype(BF16)


def tap_rows(cot_ref, side, table, even_ref, odd_ref, taps_ref):
    dout, _, ny2, nz2 = cot_ref.shape
    nz = nz2 // 2
    for b in range(nz2 // 256):
        block = cot_ref[:, side, :, 256 * b : 256 * b + 256].reshape(dout * ny2, 256)
        halves = dot(block, table)
        even_ref[b] = halves[:, :128]
        odd_ref[b] = halves[:, 128:]

    def row(y, carry):
        even = load_rows(even_ref, y, dout, ny2)
        odd = load_rows(odd_ref, y, dout, ny2)
        base = pl.multiple_of((y + 1) * 4 * dout, 4 * dout)
        pieces = (pltpu.roll(odd, 1, 1), even, odd, pltpu.roll(even, nz - 1, 1))
        for k, piece in enumerate(pieces):
            taps_ref[pl.ds(base + k * dout, dout), :] = piece.astype(BF16)
        return carry

    lax.fori_loop(0, ny2, row, 0, unroll=2)
    group = 4 * dout
    taps_ref[:group, :] = taps_ref[ny2 * group : (ny2 + 1) * group, :]
    taps_ref[(ny2 + 1) * group :, :] = taps_ref[group : 2 * group, :]


def first_kernel(
    core_ref, own_ref, inner_ref, cot_ref, w_ref,
    taps_out_ref, own_t_ref, inner_t_ref, wg_ref, vg_ref, to_inner_ref, to_outer_ref,
    wide_ref, even_ref, odd_ref, taps_in_ref,
):
    dout, _, ny2, _ = cot_ref.shape
    ny = ny2 // 2
    chans = w_ref.shape[2]
    group = 4 * dout
    (side_i, own_i, nbr_i), (side_o, own_o, nbr_o) = roles(core_ref[0])
    table = split_table()

    def grad_weights(own, nbr):
        both = jnp.concatenate([w_ref[own].astype(F32), w_ref[nbr].astype(F32)], 1)
        return both.T.astype(BF16)

    tap_rows(cot_ref, side_o, table, even_ref, odd_ref, taps_out_ref)
    weights_o = grad_weights(own_o, nbr_o)

    def outer_row(y, carry):
        taps = taps_out_ref[pl.ds(pl.multiple_of(y * 2 * group, 2 * group), 4 * group), :]
        sums = dot(weights_o, taps)
        store_rows(vg_ref, y, ny, sums[:chans])
        store_rows(to_outer_ref, y, ny, sums[chans:])
        return carry

    lax.fori_loop(0, ny, outer_row, 0)
    rows_by_y(own_ref, wide_ref, own_t_ref, ny)
    rows_by_y(inner_ref, wide_ref, inner_t_ref, ny)
    tap_rows(cot_ref, side_i, table, even_ref, odd_ref, taps_in_ref)
    weights_i = grad_weights(own_i, nbr_i)
    wg_ref[...] = jnp.zeros_like(wg_ref)

    def inner_row(y, carry):
        taps = taps_in_ref[pl.ds(pl.multiple_of(y * 2 * group, 2 * group), 4 * group), :]
        sums = dot(weights_i, taps)
        store_rows(vg_ref, y, ny, load_rows(vg_ref, y, chans, ny) + sums[:chans])
        store_rows(to_inner_ref, y, ny, sums[chans:])
        at = pl.ds(pl.multiple_of(y * chans, chans), chans)
        cells = jnp.concatenate([own_t_ref[at, :], inner_t_ref[at, :]], 0)
        wg_ref[...] += lax.dot_general(taps, cells, NT, preferred_element_type=F32)
        return carry

    lax.fori_loop(0, ny, inner_row, 0)


def second_kernel(taps_ref, own_t_ref, outer_ref, arrived_ref, sum_ref, outer_t_ref, wide_ref):
    chans = arrived_ref.shape[1] // 2
    ny = outer_ref.shape[0] // chans
    rows = sum_ref.shape[0]
    rows_by_y(outer_ref, wide_ref, outer_t_ref, ny)
    sum_ref[...] = arrived_ref[...]

    def row(y, carry):
        taps = taps_ref[pl.ds(pl.multiple_of(y * rows // 2, rows // 2), rows), :]
        at = pl.ds(pl.multiple_of(y * chans, chans), chans)
        cells = jnp.concatenate([own_t_ref[at, :], outer_t_ref[at, :]], 0)
        sum_ref[...] += lax.dot_general(taps, cells, NT, preferred_element_type=F32)
        return carry

    lax.fori_loop(0, ny, row, 0)


def fine_kernel(core_ref, own_t_ref, inner_t_ref, outer_t_ref, w_ref, out_ref, even_ref, odd_ref):
    dout, _, ny2, nz2 = out_ref.shape
    ny, nz = ny2 // 2, nz2 // 2
    chans = w_ref.shape[2]
    group = 4 * dout
    table = join_table()
    for (side, own, nbr), nbr_t_ref in zip(roles(core_ref[0]), (inner_t_ref, outer_t_ref)):
        weights = []
        for near, far in ((1, 3), (2, 0)):
            slabs = [w_ref[x, y * group : (y + 1) * group, :] for x in (own, nbr) for y in (near, far)]
            weights.append(jnp.concatenate(slabs, 1))

        def row(y, carry):
            for phase, step in ((0, ny - 1), (1, 1)):
                near = pl.ds(pl.multiple_of(y * chans, chans), chans)
                far = pl.ds(pl.multiple_of(lax.rem(y + step, ny) * chans, chans), chans)
                cells = jnp.concatenate(
                    [own_t_ref[near, :], own_t_ref[far, :], nbr_t_ref[near, :], nbr_t_ref[far, :]], 0
                )
                sums = dot(weights[phase], cells)
                even = sums[dout : 2 * dout] + pltpu.roll(sums[3 * dout :], 1, 1)
                odd = sums[2 * dout : 3 * dout] + pltpu.roll(sums[:dout], nz - 1, 1)
                store_rows(even_ref, 2 * y + phase, ny2, even)
                store_rows(odd_ref, 2 * y + phase, ny2, odd)
            return carry

        lax.fori_loop(0, ny, row, 0)
        for b in range(nz // 128):
            halves = jnp.concatenate([even_ref[b].astype(BF16), odd_ref[b].astype(BF16)], 1)
            fine = dot(halves, table).astype(BF16)
            out_ref[:, side, :, 256 * b : 256 * b + 256] = fine.reshape(dout, ny2, 256)


def last_kernel(a_ref, b_ref, c_ref, out_ref):
    for b in range(a_ref.shape[0]):
        out_ref[:, 128 * b : 128 * b + 128] = (a_ref[b] + b_ref[b] + c_ref[b]).astype(BF16)


def call(kernel, outs, scratch, in_smem, flops, moved):
    vmem = pl.BlockSpec(memory_space=pltpu.VMEM)
    smem = pl.BlockSpec(memory_space=pltpu.SMEM)
    return pl.pallas_call(
        kernel,
        out_shape=outs,
        in_specs=[smem if s else vmem for s in in_smem],
        out_specs=[vmem] * len(outs),
        scratch_shapes=scratch,
        compiler_params=pltpu.CompilerParams(vmem_limit_bytes=40 << 20),
        cost_estimate=pl.CostEstimate(flops=flops, bytes_accessed=moved, transcendentals=0),
    )


def on_device(volume, weights, cotangent):
    chans, planes, ny, nz = volume.shape
    dout = cotangent.shape[0]
    peers = lax.axis_size("gx")
    me = lax.axis_index("gx")
    core = lax.rem(me, 2)
    core_arg = core.astype(jnp.int32).reshape(1)
    inner_pairs = [(i, i ^ 1) for i in range(peers)]
    outer_pairs = [(i, (i + (1 if i % 2 else -1)) % peers) for i in range(peers)]

    own = volume.reshape(chans * ny, nz)
    outer = lax.ppermute(own, "gx", outer_pairs)
    inner = lax.ppermute(own, "gx", inner_pairs)
    kernels = jnp.transpose(weights, (0, 1, 2, 4, 3)).reshape(4, 16 * dout, chans)

    rows, wide = chans * ny, 16 * dout
    group = 4 * dout
    struct = jax.ShapeDtypeStruct
    blocks_c, blocks_d = (nz // 128, rows, 128), (nz // 128, dout * 2 * ny, 128)
    taps_o, own_t, inner_t, wg_i, vg, to_inner, to_outer = call(
        first_kernel,
        [struct(((2 * ny + 2) * group, nz), BF16), struct((rows, nz), BF16), struct((rows, nz), BF16),
         struct((wide, 2 * chans), F32), struct(blocks_c, F32), struct(blocks_c, F32), struct(blocks_c, F32)],
        [pltpu.VMEM(blocks_c, F32), pltpu.VMEM(blocks_d, F32), pltpu.VMEM(blocks_d, F32),
         pltpu.VMEM(((2 * ny + 2) * group, nz), BF16)],
        (1, 0, 0, 0, 0), 6_000_000_000, 12_000_000,
    )(core_arg, own, inner, cotangent, kernels)

    from_outer = lax.ppermute(to_outer, "gx", outer_pairs)
    from_inner = lax.ppermute(to_inner, "gx", inner_pairs)
    wg_arrived = lax.ppermute(wg_i, "gx", inner_pairs)

    total, outer_t = call(
        second_kernel,
        [struct((wide, 2 * chans), F32), struct((rows, nz), BF16)],
        [pltpu.VMEM(blocks_c, F32)],
        (0, 0, 0, 0), 1_000_000_000, 4_000_000,
    )(taps_o, own_t, outer, wg_arrived)

    (upsampled,) = call(
        fine_kernel,
        [struct(cotangent.shape, BF16)],
        [pltpu.VMEM(blocks_d, F32), pltpu.VMEM(blocks_d, F32)],
        (1, 0, 0, 0, 0), 4_000_000_000, 4_000_000,
    )(core_arg, own_t, inner_t, outer_t, kernels)

    total = sum_over_chips(total, me, peers)
    other = lax.ppermute(total, "gx", inner_pairs)
    scale = 1.0 / math.sqrt(peers * planes * ny * nz)
    mine_own, mine_nbr = total[:, :chans], total[:, chans:]
    other_own, other_nbr = other[:, :chans], other[:, chans:]
    first = core == 0
    blocks = jnp.stack(
        [
            jnp.where(first, other_nbr, mine_nbr),
            jnp.where(first, mine_own, other_own),
            jnp.where(first, other_own, mine_own),
            jnp.where(first, mine_nbr, other_nbr),
        ]
    )
    weight_grad = jnp.transpose((blocks * scale).reshape(4, 4, 4, dout, chans), (0, 1, 2, 4, 3))
    (volume_grad,) = call(last_kernel, [struct((rows, nz), BF16)], [], (0, 0, 0), 600_000, 4_000_000)(
        vg, from_inner, from_outer
    )
    volume_grad = volume_grad.reshape(volume.shape)
    return (upsampled, volume_grad, weight_grad)


def sum_over_chips(total, me, peers):
    if peers & (peers - 1) or peers < 4:
        groups = [[i for i in range(peers) if i % 2 == c] for c in range(2)]
        return lax.psum(total, "gx", axis_index_groups=groups)
    half = total.shape[0] // 2
    bit = lax.rem(me // 2, 2)
    pairs = lambda k: [(i, i ^ k) for i in range(peers)]
    mine = lax.dynamic_slice_in_dim(total, bit * half, half, 0)
    away = lax.dynamic_slice_in_dim(total, (1 - bit) * half, half, 0)
    mine = mine + lax.ppermute(away, "gx", pairs(2))
    step = 4
    while step < peers:
        mine = mine + lax.ppermute(mine, "gx", pairs(step))
        step *= 2
    away = lax.ppermute(mine, "gx", pairs(2))
    return jnp.where(bit == 0, jnp.concatenate([mine, away]), jnp.concatenate([away, mine]))


def solution(mesh):
    placed = (P(None, "gx", "groups", None), P(), P(None, "gx", "groups", None))
    return jax.shard_map(
        on_device,
        mesh=mesh,
        in_specs=placed,
        out_specs=(
            P(None, "gx", "groups", None),
            P(None, "gx", "groups", None),
            P("groups", None, None, None, None),
        ),
        check_vma=False,
    )
```

```python
import functools
import math

import jax
import jax.numpy as jnp
from jax import lax
from jax.experimental import pallas as pl
from jax.experimental.pallas import tpu as pltpu
from jax.sharding import PartitionSpec as P

F32 = jnp.float32
BF16 = jnp.bfloat16
NT = (((1,), (1,)), ((), ()))
TOP = 14.0
FLOPS_A = 500_000_000
FLOPS_B = 500_000_000


def roles(core):
    inner = (1 - core, 2 - core, 3 * core)
    outer = (core, 1 + core, 3 - 3 * core)
    return inner, outer


def dot(a, b):
    return jnp.dot(a, b, preferred_element_type=F32)


def split_table():
    row = lax.broadcasted_iota(jnp.int32, (256, 256), 0)
    col = lax.broadcasted_iota(jnp.int32, (256, 256), 1)
    return (row == jnp.where(col < 128, 2 * col, 2 * col - 255)).astype(BF16)


def join_table():
    row = lax.broadcasted_iota(jnp.int32, (256, 256), 0)
    col = lax.broadcasted_iota(jnp.int32, (256, 256), 1)
    return (col == jnp.where(row < 128, 2 * row, 2 * row - 255)).astype(BF16)


def load_rows(ref, start, count, stride):
    return jnp.concatenate([ref[b, pl.ds(start, count, stride=stride), :] for b in range(ref.shape[0])], 1)


def store_rows(ref, start, stride, value):
    for b in range(ref.shape[0]):
        ref[b, pl.ds(start, value.shape[0], stride=stride), :] = value[:, 128 * b : 128 * b + 128]


def rows_by_y(source_ref, wide_ref, target_ref, ny):
    chans = source_ref.shape[0] // ny
    for b in range(wide_ref.shape[0]):
        wide_ref[b] = source_ref[:, 128 * b : 128 * b + 128].astype(F32)
    for y in range(ny):
        target_ref[y * chans : (y + 1) * chans, :] = load_rows(wide_ref, y, chans, ny).astype(BF16)


def fetches(cot_ref, side, plane_ref, sems):
    chunk = plane_ref.shape[0] // sems.shape[0]
    return [
        pltpu.make_async_copy(
            cot_ref.at[pl.ds(chunk * i, chunk), side], plane_ref.at[pl.ds(chunk * i, chunk)], sems.at[i]
        )
        for i in range(sems.shape[0])
    ]


def tap_rows(copies, plane_ref, even_ref, odd_ref, taps_ref):
    dout, ny2, nz2 = plane_ref.shape
    nz = nz2 // 2
    table = split_table()
    chunk = dout // len(copies)
    for i, copy in enumerate(copies):
        copy.wait()
        at = pl.ds(chunk * i * ny2, chunk * ny2)
        for b in range(nz2 // 256):
            block = plane_ref[chunk * i : chunk * i + chunk, :, 256 * b : 256 * b + 256]
            halves = dot(block.reshape(chunk * ny2, 256), table)
            even_ref[b, at, :] = halves[:, :128]
            odd_ref[b, at, :] = halves[:, 128:]

    def row(y, carry):
        even = load_rows(even_ref, y, dout, ny2)
        odd = load_rows(odd_ref, y, dout, ny2)
        base = pl.multiple_of((y + 1) * 4 * dout, 4 * dout)
        pieces = (pltpu.roll(odd, 1, 1), even, odd, pltpu.roll(even, nz - 1, 1))
        for k, piece in enumerate(pieces):
            taps_ref[pl.ds(base + k * dout, dout), :] = piece.astype(BF16)
        return carry

    lax.fori_loop(0, ny2, row, 0, unroll=4)
    group = 4 * dout
    taps_ref[:group, :] = taps_ref[ny2 * group : (ny2 + 1) * group, :]
    taps_ref[(ny2 + 1) * group :, :] = taps_ref[group : 2 * group, :]


def grad_weights(w_ref, own, nbr):
    both = jnp.concatenate([w_ref[own].astype(F32), w_ref[nbr].astype(F32)], 1)
    return both.T.astype(BF16)


def flatten(blocks_ref, out_ref):
    for b in range(blocks_ref.shape[0]):
        out_ref[:, 128 * b : 128 * b + 128] = blocks_ref[b]


def outer_kernel(
    core_ref, cot_ref, w_ref, taps_ref, vg_ref, partial_ref,
    plane_ref, even_ref, odd_ref, vg_blocks, partial_blocks, sems,
):
    dout, ny2, _ = plane_ref.shape
    ny, group, chans = ny2 // 2, 4 * dout, w_ref.shape[2]
    side, own, nbr = roles(core_ref[0])[1]
    copies = fetches(cot_ref, side, plane_ref, sems)
    for copy in copies:
        copy.start()
    weights = grad_weights(w_ref, own, nbr)
    tap_rows(copies, plane_ref, even_ref, odd_ref, taps_ref)
    most = jnp.zeros((chans, vg_ref.shape[1]), F32)
    for y in range(ny):
        sums = dot(weights, taps_ref[y * 2 * group : (y * 2 + 4) * group, :])
        store_rows(vg_blocks, y, ny, sums[:chans])
        store_rows(partial_blocks, y, ny, sums[chans:])
        most = jnp.maximum(most, jnp.abs(sums[chans:]))
    flatten(vg_blocks, vg_ref)
    rows = chans * ny
    most = jnp.max(jnp.max(most, axis=0, keepdims=True), axis=1, keepdims=True)
    level = jnp.ceil(jnp.log2(jnp.maximum(most, 1e-30)))
    shrink = jnp.exp2(TOP - level)
    for b in range(partial_blocks.shape[0]):
        partial_ref[:rows, 128 * b : 128 * b + 128] = partial_blocks[b] * shrink
    partial_ref[rows:, :] = jnp.broadcast_to(level, (partial_ref.shape[0] - rows, partial_ref.shape[1]))


def inner_kernel(
    core_ref, cot_ref, w_ref, own_ref, inner_ref, vg_part_ref,
    own_t_ref, inner_t_ref, wg_ref, vg_ref, partial_ref,
    plane_ref, even_ref, odd_ref, vg_blocks, partial_blocks, taps_ref, sems,
):
    dout, ny2, _ = plane_ref.shape
    ny, group, chans = ny2 // 2, 4 * dout, w_ref.shape[2]
    side, own, nbr = roles(core_ref[0])[0]
    copies = fetches(cot_ref, side, plane_ref, sems)
    for copy in copies:
        copy.start()
    rows_by_y(own_ref, vg_blocks, own_t_ref, ny)
    rows_by_y(inner_ref, partial_blocks, inner_t_ref, ny)
    weights = grad_weights(w_ref, own, nbr)
    tap_rows(copies, plane_ref, even_ref, odd_ref, taps_ref)
    for y in range(ny):
        taps = taps_ref[y * 2 * group : (y * 2 + 4) * group, :]
        sums = dot(weights, taps)
        store_rows(vg_blocks, y, ny, sums[:chans])
        store_rows(partial_blocks, y, ny, sums[chans:])
        cells = jnp.concatenate([r[y * chans : (y + 1) * chans, :] for r in (own_t_ref, inner_t_ref)], 0)
        grads = lax.dot_general(taps, cells, NT, preferred_element_type=F32)
        wg_ref[...] = grads if y == 0 else wg_ref[...] + grads
    for b in range(vg_blocks.shape[0]):
        at = slice(128 * b, 128 * b + 128)
        vg_ref[:, at] = vg_part_ref[:, at] + vg_blocks[b]
    flatten(partial_blocks, partial_ref)


def split(bit, whole_ref, keep_ref, send_ref):
    half = keep_ref.shape[0]
    keep_ref[...] = whole_ref[pl.ds(pl.multiple_of(bit * half, half), half), :]
    send_ref[...] = whole_ref[pl.ds(pl.multiple_of((1 - bit) * half, half), half), :]


def second_kernel(bits_ref, taps_ref, own_t_ref, outer_ref, arrived_ref, keep_ref, send_ref, outer_t_ref, wide_ref, sum_ref):
    chans = arrived_ref.shape[1] // 2
    ny = outer_ref.shape[0] // chans
    rows = sum_ref.shape[0]
    rows_by_y(outer_ref, wide_ref, outer_t_ref, ny)
    for y in range(ny):
        taps = taps_ref[y * rows // 2 : y * rows // 2 + rows, :]
        cells = jnp.concatenate([r[y * chans : (y + 1) * chans, :] for r in (own_t_ref, outer_t_ref)], 0)
        grads = lax.dot_general(taps, cells, NT, preferred_element_type=F32)
        sum_ref[...] = (arrived_ref if y == 0 else sum_ref)[...] + grads
    split(bits_ref[1], sum_ref, keep_ref, send_ref)


def add_split_kernel(which, bits_ref, a_ref, b_ref, keep_ref, send_ref, sum_ref):
    sum_ref[...] = a_ref[...] + b_ref[...]
    split(bits_ref[which], sum_ref, keep_ref, send_ref)


def add_kernel(a_ref, b_ref, out_ref):
    out_ref[...] = a_ref[...] + b_ref[...]


def join_kernel(which, bits_ref, mine_ref, there_ref, out_ref):
    bit, half = bits_ref[which], mine_ref.shape[0]
    out_ref[pl.ds(pl.multiple_of(bit * half, half), half), :] = mine_ref[...]
    out_ref[pl.ds(pl.multiple_of((1 - bit) * half, half), half), :] = there_ref[...]


def taps_kernel(scale, bits_ref, mine_ref, other_ref, out_ref):
    chans = out_ref.shape[2]
    core = bits_ref[0]
    for ref, side in ((mine_ref, core), (other_ref, 1 - core)):
        _, own, nbr = roles(side)[1]
        both = ref[...] * scale
        out_ref[own] = both[:, :chans]
        out_ref[nbr] = both[:, chans:]


def cells_kernel(vg_ref, inner_ref, outer_ref, out_ref):
    rows = vg_ref.shape[0]
    grow = jnp.exp2(outer_ref[rows : rows + 1, :] - TOP)
    out_ref[...] = (vg_ref[...] + inner_ref[...] + outer_ref[:rows, :] * grow).astype(BF16)


def fine_kernel(which, core_ref, own_t_ref, nbr_t_ref, w_ref, *refs):
    out_ref, plane_ref, even_ref, odd_ref, sem = refs[-5:]
    dout, ny2, nz2 = plane_ref.shape
    ny, nz = ny2 // 2, nz2 // 2
    chans = w_ref.shape[2]
    group = 4 * dout
    side, own, nbr = roles(core_ref[0])[which]
    for phase, step, taps in ((0, ny - 1, (1, 3)), (1, 1, (2, 0))):
        slabs = [w_ref[x, y * group : (y + 1) * group, :] for x in (own, nbr) for y in taps]
        weights = jnp.concatenate(slabs, 1)
        for y in range(ny):
            near = slice(y * chans, (y + 1) * chans)
            far = slice((y + step) % ny * chans, ((y + step) % ny + 1) * chans)
            cells = jnp.concatenate([r[at, :] for r in (own_t_ref, nbr_t_ref) for at in (near, far)], 0)
            sums = dot(weights, cells)
            even = sums[dout : 2 * dout] + pltpu.roll(sums[3 * dout :], 1, 1)
            odd = sums[2 * dout : 3 * dout] + pltpu.roll(sums[:dout], nz - 1, 1)
            store_rows(even_ref, 2 * y + phase, ny2, even)
            store_rows(odd_ref, 2 * y + phase, ny2, odd)
    table = join_table()
    for b in range(nz // 128):
        halves = jnp.concatenate([even_ref[b].astype(BF16), odd_ref[b].astype(BF16)], 1)
        fine = dot(halves, table).astype(BF16)
        plane_ref[:, :, 256 * b : 256 * b + 256] = fine.reshape(dout, ny2, 256)
    copy = pltpu.make_async_copy(plane_ref, out_ref.at[:, side], sem)
    copy.start()
    copy.wait()


VMEM = pl.BlockSpec(memory_space=pltpu.VMEM)
SMEM = pl.BlockSpec(memory_space=pltpu.SMEM)
HBM = pl.BlockSpec(memory_space=pltpu.HBM)


def call(kernel, in_specs, out_specs, outs, scratch, grant, flops=1_000, **more):
    return pl.pallas_call(
        kernel,
        out_shape=outs,
        in_specs=in_specs,
        out_specs=out_specs,
        scratch_shapes=scratch,
        compiler_params=pltpu.CompilerParams(vmem_limit_bytes=grant << 20),
        cost_estimate=pl.CostEstimate(flops=flops, bytes_accessed=1_000, transcendentals=0),
        **more,
    )


def together(*values):
    return lax.optimization_barrier(values)


def on_device(volume, weights, cotangent):
    chans, planes, ny, nz = volume.shape
    dout = cotangent.shape[0]
    peers = lax.axis_size("gx")
    me = lax.axis_index("gx")
    bits = jnp.stack([me & 1, (me >> 2) & 1, (me >> 1) & 1]).astype(jnp.int32)
    rows, wide, group = chans * ny, 16 * dout, 4 * dout
    struct = jax.ShapeDtypeStruct
    blocks_c, blocks_d = (nz // 128, rows, 128), (nz // 128, dout * 2 * ny, 128)
    taps_shape, plane_shape = ((2 * ny + 2) * group, nz), (dout, 2 * ny, 2 * nz)
    cells, wide_cells = struct((rows, nz), BF16), struct((rows, nz), F32)
    work = [pltpu.VMEM(plane_shape, BF16), pltpu.VMEM(blocks_d, F32), pltpu.VMEM(blocks_d, F32)]
    chunks = pltpu.SemaphoreType.DMA((4,))

    def swap(value, k):
        return lax.ppermute(value, "gx", [(i, i ^ k) for i in range(peers)])

    def beyond(value):
        return lax.ppermute(value, "gx", [(i, (i + (1 if i % 2 else -1)) % peers) for i in range(peers)])

    cotangent = pltpu.with_memory_space_constraint(cotangent, pltpu.HBM)
    own = volume.reshape(rows, nz)
    outer = beyond(own)
    inner = swap(own, 1)
    kernels = jnp.transpose(weights, (0, 1, 2, 4, 3)).reshape(4, wide, chans)

    taps_o, vg_o, to_outer = call(
        outer_kernel,
        [SMEM, HBM, VMEM],
        [VMEM] * 3,
        [struct(taps_shape, BF16), wide_cells, struct((rows + 16, nz), F32)],
        work + [pltpu.VMEM(blocks_c, F32), pltpu.VMEM(blocks_c, F32), chunks],
        8,
    )(bits, cotangent, kernels)
    to_outer, vg_o = together(to_outer.astype(jnp.float16), vg_o)
    from_outer = beyond(to_outer)

    own_t, inner_t, wg_i, vg, to_inner = call(
        inner_kernel,
        [SMEM, HBM] + [VMEM] * 4,
        [VMEM] * 5,
        [cells, cells, struct((wide, 2 * chans), F32), wide_cells, wide_cells],
        work + [pltpu.VMEM(blocks_c, F32), pltpu.VMEM(blocks_c, F32), pltpu.VMEM(taps_shape, BF16), chunks],
        12,
    )(bits, cotangent, kernels, own, inner, vg_o)
    wg_arrived = swap(wg_i, 1)

    def piece(n):
        return struct((wide // n, 2 * chans), F32)

    keep, send, outer_t = call(
        second_kernel,
        [SMEM] + [VMEM] * 4,
        [VMEM] * 3,
        [piece(2), piece(2), cells],
        [pltpu.VMEM(blocks_c, F32), pltpu.VMEM((wide, 2 * chans), F32)],
        6,
        flops=FLOPS_A,
    )(bits, taps_o, own_t, outer, wg_arrived)

    def fine(which, nbr_t, so_far):
        more = {} if so_far is None else {"input_output_aliases": {4: 0}}
        return call(
            functools.partial(fine_kernel, which),
            [SMEM, VMEM, VMEM, VMEM] + [HBM] * (so_far is not None),
            [HBM],
            [struct(cotangent.shape, BF16)],
            work + [pltpu.SemaphoreType.DMA],
            8,
            flops=FLOPS_B,
            **more,
        )(bits, own_t, nbr_t, kernels, *([] if so_far is None else [so_far]))[0]

    def add(a, b):
        return call(add_kernel, [VMEM] * 2, [VMEM], [struct(a.shape, F32)], [], 2)(a, b)[0]

    def add_split(which, a, b):
        half = struct((a.shape[0] // 2, a.shape[1]), F32)
        return call(
            functools.partial(add_split_kernel, which),
            [SMEM, VMEM, VMEM], [VMEM] * 2, [half, half], [pltpu.VMEM(a.shape, F32)], 2,
        )(bits, a, b)

    def join(which, a, b):
        whole = struct((2 * a.shape[0], a.shape[1]), F32)
        return call(functools.partial(join_kernel, which), [SMEM, VMEM, VMEM], [VMEM], [whole], [], 2)(bits, a, b)[0]

    inner_t, keep = together(inner_t, keep)
    upsampled = fine(0, inner_t, None)
    send, to_inner, upsampled, from_outer = together(send, to_inner, upsampled, from_outer)
    from_inner = swap(to_inner, 1)
    if peers & (peers - 1) or peers < 8:
        groups = [[i for i in range(peers) if i % 2 == c] for c in range(2)]
        total = lax.psum(join(1, keep, send), "gx", axis_index_groups=groups)
        upsampled = fine(1, outer_t, upsampled)
        (volume_grad,) = call(cells_kernel, [VMEM] * 3, [VMEM], [cells], [], 4)(vg, from_inner, from_outer.astype(F32))
    else:
        keep, send = add_split(2, keep, swap(send, 4))
        (volume_grad,) = call(cells_kernel, [VMEM] * 3, [VMEM], [cells], [], 4)(vg, from_inner, from_outer.astype(F32))
        send, volume_grad = together(send, volume_grad)
        mine = add(keep, swap(send, 2))
        mine, outer_t = together(mine, outer_t)
        upsampled = fine(1, outer_t, upsampled)
        for k in range(3, peers.bit_length() - 1):
            mine = add(mine, swap(mine, 1 << k))
        mine, upsampled = together(mine, upsampled)
        mine = join(2, mine, swap(mine, 2))
        total = join(1, mine, swap(mine, 4))
    scale = 1.0 / math.sqrt(peers * planes * ny * nz)
    (weight_grad,) = call(
        functools.partial(taps_kernel, scale), [SMEM, VMEM, VMEM], [VMEM], [struct((4, wide, chans), F32)], [], 4
    )(bits, total, swap(total, 1))
    weight_grad = jnp.transpose(weight_grad.reshape(4, 4, 4, dout, chans), (0, 1, 2, 4, 3))
    return (upsampled, volume_grad.reshape(volume.shape), weight_grad)


def solution(mesh):
    placed = (P(None, "gx", "groups", None), P(), P(None, "gx", "groups", None))
    return jax.shard_map(
        on_device,
        mesh=mesh,
        in_specs=placed,
        out_specs=(
            P(None, "gx", "groups", None),
            P(None, "gx", "groups", None),
            P("groups", None, None, None, None),
        ),
        check_vma=False,
    )
```

```python
import functools
import math

import jax
import jax.numpy as jnp
from jax import lax
from jax.experimental import pallas as pl
from jax.experimental.pallas import tpu as pltpu
from jax.sharding import PartitionSpec as P

F32 = jnp.float32
BF16 = jnp.bfloat16
NT = (((1,), (1,)), ((), ()))
TOP = 14.0
COSTS = (1_000, 1_000, 1_000, 500_000_000, 500_000_000)


def roles(core):
    inner = (1 - core, 2 - core, 3 * core)
    outer = (core, 1 + core, 3 - 3 * core)
    return inner, outer


def dot(a, b):
    return jnp.dot(a, b, preferred_element_type=F32)


def split_table():
    row = lax.broadcasted_iota(jnp.int32, (256, 256), 0)
    col = lax.broadcasted_iota(jnp.int32, (256, 256), 1)
    return (row == jnp.where(col < 128, 2 * col, 2 * col - 255)).astype(BF16)


def join_table():
    row = lax.broadcasted_iota(jnp.int32, (256, 256), 0)
    col = lax.broadcasted_iota(jnp.int32, (256, 256), 1)
    return (col == jnp.where(row < 128, 2 * row, 2 * row - 255)).astype(BF16)


def load_rows(ref, start, count, stride):
    return jnp.concatenate([ref[b, pl.ds(start, count, stride=stride), :] for b in range(ref.shape[0])], 1)


def store_rows(ref, start, stride, value):
    for b in range(ref.shape[0]):
        ref[b, pl.ds(start, value.shape[0], stride=stride), :] = value[:, 128 * b : 128 * b + 128]


def rows_by_y(source_ref, wide_ref, target_ref, ny):
    chans = source_ref.shape[0] // ny
    for b in range(wide_ref.shape[0]):
        wide_ref[b] = source_ref[:, 128 * b : 128 * b + 128].astype(F32)
    for y in range(ny):
        target_ref[y * chans : (y + 1) * chans, :] = load_rows(wide_ref, y, chans, ny).astype(BF16)


def fetches(cot_ref, side, plane_ref, sems):
    chunk = plane_ref.shape[0] // sems.shape[0]
    return [
        pltpu.make_async_copy(
            cot_ref.at[pl.ds(chunk * i, chunk), side], plane_ref.at[pl.ds(chunk * i, chunk)], sems.at[i]
        )
        for i in range(sems.shape[0])
    ]


def tap_rows(copies, plane_ref, even_ref, odd_ref, taps_ref):
    dout, ny2, nz2 = plane_ref.shape
    nz = nz2 // 2
    table = split_table()
    chunk = dout // len(copies)
    for i, copy in enumerate(copies):
        copy.wait()
        at = pl.ds(chunk * i * ny2, chunk * ny2)
        for b in range(nz2 // 256):
            block = plane_ref[chunk * i : chunk * i + chunk, :, 256 * b : 256 * b + 256]
            halves = dot(block.reshape(chunk * ny2, 256), table)
            even_ref[b, at, :] = halves[:, :128]
            odd_ref[b, at, :] = halves[:, 128:]

    def row(y, carry):
        even = load_rows(even_ref, y, dout, ny2)
        odd = load_rows(odd_ref, y, dout, ny2)
        base = pl.multiple_of((y + 1) * 4 * dout, 4 * dout)
        pieces = (pltpu.roll(odd, 1, 1), even, odd, pltpu.roll(even, nz - 1, 1))
        for k, piece in enumerate(pieces):
            taps_ref[pl.ds(base + k * dout, dout), :] = piece.astype(BF16)
        return carry

    lax.fori_loop(0, ny2, row, 0, unroll=4)
    group = 4 * dout
    taps_ref[:group, :] = taps_ref[ny2 * group : (ny2 + 1) * group, :]
    taps_ref[(ny2 + 1) * group :, :] = taps_ref[group : 2 * group, :]


def grad_weights(w_ref, own, nbr):
    both = jnp.concatenate([w_ref[own].astype(F32), w_ref[nbr].astype(F32)], 1)
    return both.T.astype(BF16)


def flatten(blocks_ref, out_ref):
    for b in range(blocks_ref.shape[0]):
        out_ref[:, 128 * b : 128 * b + 128] = blocks_ref[b]


def outer_kernel(
    core_ref, cot_ref, w_ref, taps_ref, vg_ref, partial_ref,
    plane_ref, even_ref, odd_ref, vg_blocks, partial_blocks, sems,
):
    dout, ny2, _ = plane_ref.shape
    ny, group, chans = ny2 // 2, 4 * dout, w_ref.shape[2]
    side, own, nbr = roles(core_ref[0])[1]
    copies = fetches(cot_ref, side, plane_ref, sems)
    for copy in copies:
        copy.start()
    weights = grad_weights(w_ref, own, nbr)
    tap_rows(copies, plane_ref, even_ref, odd_ref, taps_ref)
    most = jnp.zeros((chans, vg_ref.shape[1]), F32)
    for y in range(ny):
        sums = dot(weights, taps_ref[y * 2 * group : (y * 2 + 4) * group, :])
        store_rows(vg_blocks, y, ny, sums[:chans])
        store_rows(partial_blocks, y, ny, sums[chans:])
        most = jnp.maximum(most, jnp.abs(sums[chans:]))
    flatten(vg_blocks, vg_ref)
    rows = chans * ny
    most = jnp.max(jnp.max(most, axis=0, keepdims=True), axis=1, keepdims=True)
    level = jnp.ceil(jnp.log2(jnp.maximum(most, 1e-30)))
    shrink = jnp.exp2(TOP - level)
    for b in range(partial_blocks.shape[0]):
        partial_ref[:rows, 128 * b : 128 * b + 128] = partial_blocks[b] * shrink
    partial_ref[rows:, :] = jnp.broadcast_to(level, (partial_ref.shape[0] - rows, partial_ref.shape[1]))


def inner_kernel(
    core_ref, cot_ref, w_ref, vg_part_ref, taps_ref, vg_ref, partial_ref,
    plane_ref, even_ref, odd_ref, vg_blocks, partial_blocks, sems,
):
    dout, ny2, _ = plane_ref.shape
    ny, group, chans = ny2 // 2, 4 * dout, w_ref.shape[2]
    side, own, nbr = roles(core_ref[0])[0]
    copies = fetches(cot_ref, side, plane_ref, sems)
    for copy in copies:
        copy.start()
    weights = grad_weights(w_ref, own, nbr)
    tap_rows(copies, plane_ref, even_ref, odd_ref, taps_ref)
    for y in range(ny):
        sums = dot(weights, taps_ref[y * 2 * group : (y * 2 + 4) * group, :])
        store_rows(vg_blocks, y, ny, sums[:chans])
        store_rows(partial_blocks, y, ny, sums[chans:])
    for b in range(vg_blocks.shape[0]):
        at = slice(128 * b, 128 * b + 128)
        vg_ref[:, at] = vg_part_ref[:, at] + vg_blocks[b]
    flatten(partial_blocks, partial_ref)


def tap_sums(taps_ref, own_t_ref, nbr_t_ref, sum_ref, before_ref):
    rows, chans = sum_ref.shape[0], sum_ref.shape[1] // 2
    for y in range(own_t_ref.shape[0] // chans):
        taps = taps_ref[y * rows // 2 : y * rows // 2 + rows, :]
        cells = jnp.concatenate([r[y * chans : (y + 1) * chans, :] for r in (own_t_ref, nbr_t_ref)], 0)
        grads = lax.dot_general(taps, cells, NT, preferred_element_type=F32)
        before = before_ref if y == 0 else sum_ref
        sum_ref[...] = grads if before is None else before[...] + grads


def inner_sums_kernel(taps_ref, own_ref, inner_ref, own_t_ref, inner_t_ref, wg_ref, wide_ref):
    ny = own_ref.shape[0] * 2 // wg_ref.shape[1]
    rows_by_y(own_ref, wide_ref, own_t_ref, ny)
    rows_by_y(inner_ref, wide_ref, inner_t_ref, ny)
    tap_sums(taps_ref, own_t_ref, inner_t_ref, wg_ref, None)


def split(bit, whole_ref, keep_ref, send_ref):
    half = keep_ref.shape[0]
    keep_ref[...] = whole_ref[pl.ds(pl.multiple_of(bit * half, half), half), :]
    send_ref[...] = whole_ref[pl.ds(pl.multiple_of((1 - bit) * half, half), half), :]


def outer_sums_kernel(
    bits_ref, taps_ref, own_t_ref, outer_ref, arrived_ref, keep_ref, send_ref, outer_t_ref, wide_ref, sum_ref
):
    ny = outer_ref.shape[0] * 2 // arrived_ref.shape[1]
    rows_by_y(outer_ref, wide_ref, outer_t_ref, ny)
    tap_sums(taps_ref, own_t_ref, outer_t_ref, sum_ref, arrived_ref)
    split(bits_ref[1], sum_ref, keep_ref, send_ref)


def add_split_kernel(which, bits_ref, a_ref, b_ref, keep_ref, send_ref, sum_ref):
    sum_ref[...] = a_ref[...] + b_ref[...]
    split(bits_ref[which], sum_ref, keep_ref, send_ref)


def add_kernel(a_ref, b_ref, out_ref):
    out_ref[...] = a_ref[...] + b_ref[...]


def join_kernel(which, bits_ref, mine_ref, there_ref, out_ref):
    bit, half = bits_ref[which], mine_ref.shape[0]
    out_ref[pl.ds(pl.multiple_of(bit * half, half), half), :] = mine_ref[...]
    out_ref[pl.ds(pl.multiple_of((1 - bit) * half, half), half), :] = there_ref[...]


def taps_kernel(scale, bits_ref, mine_ref, other_ref, out_ref):
    chans = out_ref.shape[2]
    core = bits_ref[0]
    for ref, side in ((mine_ref, core), (other_ref, 1 - core)):
        _, own, nbr = roles(side)[1]
        both = ref[...] * scale
        out_ref[own] = both[:, :chans]
        out_ref[nbr] = both[:, chans:]


def cells_kernel(vg_ref, inner_ref, outer_ref, out_ref):
    rows = vg_ref.shape[0]
    grow = jnp.exp2(outer_ref[rows : rows + 1, :] - TOP)
    out_ref[...] = (vg_ref[...] + inner_ref[...] + outer_ref[:rows, :] * grow).astype(BF16)


def fine_kernel(which, core_ref, own_t_ref, nbr_t_ref, w_ref, *refs):
    out_ref, plane_ref, even_ref, odd_ref, sem = refs[-5:]
    dout, ny2, nz2 = plane_ref.shape
    ny, nz = ny2 // 2, nz2 // 2
    chans = w_ref.shape[2]
    group = 4 * dout
    side, own, nbr = roles(core_ref[0])[which]
    for phase, step, taps in ((0, ny - 1, (1, 3)), (1, 1, (2, 0))):
        slabs = [w_ref[x, y * group : (y + 1) * group, :] for x in (own, nbr) for y in taps]
        weights = jnp.concatenate(slabs, 1)
        for y in range(ny):
            near = slice(y * chans, (y + 1) * chans)
            far = slice((y + step) % ny * chans, ((y + step) % ny + 1) * chans)
            cells = jnp.concatenate([r[at, :] for r in (own_t_ref, nbr_t_ref) for at in (near, far)], 0)
            sums = dot(weights, cells)
            even = sums[dout : 2 * dout] + pltpu.roll(sums[3 * dout :], 1, 1)
            odd = sums[2 * dout : 3 * dout] + pltpu.roll(sums[:dout], nz - 1, 1)
            store_rows(even_ref, 2 * y + phase, ny2, even)
            store_rows(odd_ref, 2 * y + phase, ny2, odd)
    table = join_table()
    for b in range(nz // 128):
        halves = jnp.concatenate([even_ref[b].astype(BF16), odd_ref[b].astype(BF16)], 1)
        fine = dot(halves, table).astype(BF16)
        plane_ref[:, :, 256 * b : 256 * b + 256] = fine.reshape(dout, ny2, 256)
    copy = pltpu.make_async_copy(plane_ref, out_ref.at[:, side], sem)
    copy.start()
    copy.wait()


VMEM = pl.BlockSpec(memory_space=pltpu.VMEM)
SMEM = pl.BlockSpec(memory_space=pltpu.SMEM)
HBM = pl.BlockSpec(memory_space=pltpu.HBM)


def call(kernel, in_specs, out_specs, outs, scratch, grant, flops=1_000, **more):
    return pl.pallas_call(
        kernel,
        out_shape=outs,
        in_specs=in_specs,
        out_specs=out_specs,
        scratch_shapes=scratch,
        compiler_params=pltpu.CompilerParams(vmem_limit_bytes=grant << 20),
        cost_estimate=pl.CostEstimate(flops=flops, bytes_accessed=1_000, transcendentals=0),
        **more,
    )


def together(*values):
    return lax.optimization_barrier(values)


def on_device(volume, weights, cotangent):
    chans, planes, ny, nz = volume.shape
    dout = cotangent.shape[0]
    peers = lax.axis_size("gx")
    me = lax.axis_index("gx")
    bits = jnp.stack([me & 1, (me >> 2) & 1, (me >> 1) & 1]).astype(jnp.int32)
    rows, wide, group = chans * ny, 16 * dout, 4 * dout
    struct = jax.ShapeDtypeStruct
    blocks_c, blocks_d = (nz // 128, rows, 128), (nz // 128, dout * 2 * ny, 128)
    taps_shape, plane_shape = ((2 * ny + 2) * group, nz), (dout, 2 * ny, 2 * nz)
    cells, wide_cells = struct((rows, nz), BF16), struct((rows, nz), F32)
    work = [pltpu.VMEM(plane_shape, BF16), pltpu.VMEM(blocks_d, F32), pltpu.VMEM(blocks_d, F32)]
    chunks = pltpu.SemaphoreType.DMA((4,))

    def swap(value, k):
        return lax.ppermute(value, "gx", [(i, i ^ k) for i in range(peers)])

    def beyond(value):
        return lax.ppermute(value, "gx", [(i, (i + (1 if i % 2 else -1)) % peers) for i in range(peers)])

    cotangent = pltpu.with_memory_space_constraint(cotangent, pltpu.HBM)
    own = volume.reshape(rows, nz)
    outer = beyond(own)
    inner = swap(own, 1)
    kernels = jnp.transpose(weights, (0, 1, 2, 4, 3)).reshape(4, wide, chans)

    taps_o, vg_o, to_outer = call(
        outer_kernel,
        [SMEM, HBM, VMEM],
        [VMEM] * 3,
        [struct(taps_shape, BF16), wide_cells, struct((rows + 16, nz), F32)],
        work + [pltpu.VMEM(blocks_c, F32), pltpu.VMEM(blocks_c, F32), chunks],
        8,
        flops=COSTS[0],
    )(bits, cotangent, kernels)
    to_outer = to_outer.astype(jnp.float16)

    taps_i, vg, to_inner = call(
        inner_kernel,
        [SMEM, HBM, VMEM, VMEM],
        [VMEM] * 3,
        [struct(taps_shape, BF16), wide_cells, wide_cells],
        work + [pltpu.VMEM(blocks_c, F32), pltpu.VMEM(blocks_c, F32), chunks],
        8,
        flops=COSTS[1],
    )(bits, cotangent, kernels, vg_o)
    to_outer, taps_i = together(to_outer, taps_i)
    from_outer = beyond(to_outer)
    own_t, inner_t, wg_i = call(
        inner_sums_kernel,
        [VMEM] * 3,
        [VMEM] * 3,
        [cells, cells, struct((wide, 2 * chans), F32)],
        [pltpu.VMEM(blocks_c, F32)],
        4,
        flops=COSTS[2],
    )(taps_i, own, inner)
    wg_arrived = swap(wg_i, 1)

    def piece(n):
        return struct((wide // n, 2 * chans), F32)

    keep, send, outer_t = call(
        outer_sums_kernel,
        [SMEM] + [VMEM] * 4,
        [VMEM] * 3,
        [piece(2), piece(2), cells],
        [pltpu.VMEM(blocks_c, F32), pltpu.VMEM((wide, 2 * chans), F32)],
        6,
        flops=COSTS[3],
    )(bits, taps_o, own_t, outer, wg_arrived)

    def fine(which, nbr_t, so_far):
        more = {} if so_far is None else {"input_output_aliases": {4: 0}}
        return call(
            functools.partial(fine_kernel, which),
            [SMEM, VMEM, VMEM, VMEM] + [HBM] * (so_far is not None),
            [HBM],
            [struct(cotangent.shape, BF16)],
            work + [pltpu.SemaphoreType.DMA],
            8,
            flops=COSTS[4],
            **more,
        )(bits, own_t, nbr_t, kernels, *([] if so_far is None else [so_far]))[0]

    def add(a, b):
        return call(add_kernel, [VMEM] * 2, [VMEM], [struct(a.shape, F32)], [], 2)(a, b)[0]

    def add_split(which, a, b):
        half = struct((a.shape[0] // 2, a.shape[1]), F32)
        return call(
            functools.partial(add_split_kernel, which),
            [SMEM, VMEM, VMEM], [VMEM] * 2, [half, half], [pltpu.VMEM(a.shape, F32)], 2,
        )(bits, a, b)

    def join(which, a, b):
        whole = struct((2 * a.shape[0], a.shape[1]), F32)
        return call(functools.partial(join_kernel, which), [SMEM, VMEM, VMEM], [VMEM], [whole], [], 2)(bits, a, b)[0]

    def cell_grads(from_inner, from_outer):
        return call(cells_kernel, [VMEM] * 3, [VMEM], [cells], [], 4)(vg, from_inner, from_outer)[0]

    send, inner_t = together(send, inner_t)
    upsampled = fine(0, inner_t, None)
    if peers & (peers - 1) or peers < 8:
        groups = [[i for i in range(peers) if i % 2 == c] for c in range(2)]
        total = lax.psum(join(1, keep, send), "gx", axis_index_groups=groups)
        upsampled = fine(1, outer_t, upsampled)
        volume_grad = cell_grads(swap(to_inner, 1), from_outer.astype(F32))
    else:
        keep, send = add_split(2, keep, swap(send, 4))
        send, upsampled, from_outer = together(send, upsampled, from_outer)
        mine = add(keep, swap(send, 2))
        mine, outer_t, to_inner, from_outer = together(mine, outer_t, to_inner, from_outer)
        upsampled = fine(1, outer_t, upsampled)
        from_inner, from_outer = swap(to_inner, 1), from_outer.astype(F32)
        for k in range(3, peers.bit_length() - 1):
            mine = add(mine, swap(mine, 1 << k))
        mine, upsampled, from_inner, from_outer = together(mine, upsampled, from_inner, from_outer)
        volume_grad = cell_grads(from_inner, from_outer)
        mine = join(2, mine, swap(mine, 2))
        mine, volume_grad = together(mine, volume_grad)
        total = join(1, mine, swap(mine, 4))
    scale = 1.0 / math.sqrt(peers * planes * ny * nz)
    (weight_grad,) = call(
        functools.partial(taps_kernel, scale), [SMEM, VMEM, VMEM], [VMEM], [struct((4, wide, chans), F32)], [], 4
    )(bits, total, swap(total, 1))
    weight_grad = jnp.transpose(weight_grad.reshape(4, 4, 4, dout, chans), (0, 1, 2, 4, 3))
    return (upsampled, volume_grad.reshape(volume.shape), weight_grad)


def solution(mesh):
    placed = (P(None, "gx", "groups", None), P(), P(None, "gx", "groups", None))
    return jax.shard_map(
        on_device,
        mesh=mesh,
        in_specs=placed,
        out_specs=(
            P(None, "gx", "groups", None),
            P(None, "gx", "groups", None),
            P("groups", None, None, None, None),
        ),
        check_vma=False,
    )
```

```python
import functools
import math

import jax
import jax.numpy as jnp
from jax import lax
from jax.experimental import pallas as pl
from jax.experimental.pallas import tpu as pltpu
from jax.sharding import PartitionSpec as P

F32 = jnp.float32
BF16 = jnp.bfloat16
F16 = jnp.float16
NT = (((1,), (1,)), ((), ()))
TOP = 14.0
TAIL = 16
COSTS = (1_000, 1_000, 1_000, 1_000, 500_000_000)


def roles(core):
    inner = (1 - core, 2 - core, 3 * core)
    outer = (core, 1 + core, 3 - 3 * core)
    return inner, outer


def level_of(most):
    return jnp.ceil(jnp.log2(jnp.maximum(jnp.max(most, axis=1, keepdims=True), 1e-30)))


def shrink_into(value, out_ref):
    level = level_of(jnp.max(jnp.abs(value), axis=0, keepdims=True))
    out_ref[: value.shape[0], :] = value * jnp.exp2(TOP - level)
    out_ref[value.shape[0] :, :] = jnp.broadcast_to(level, (TAIL, value.shape[1]))


def grown(ref):
    rows = ref.shape[0] - TAIL
    return ref[:rows, :] * jnp.exp2(ref[rows : rows + 1, :] - TOP)


def dot(a, b):
    return jnp.dot(a, b, preferred_element_type=F32)


def split_table():
    row = lax.broadcasted_iota(jnp.int32, (256, 256), 0)
    col = lax.broadcasted_iota(jnp.int32, (256, 256), 1)
    return (row == jnp.where(col < 128, 2 * col, 2 * col - 255)).astype(BF16)


def join_table():
    row = lax.broadcasted_iota(jnp.int32, (256, 256), 0)
    col = lax.broadcasted_iota(jnp.int32, (256, 256), 1)
    return (col == jnp.where(row < 128, 2 * row, 2 * row - 255)).astype(BF16)


def load_rows(ref, start, count, stride):
    return jnp.concatenate([ref[b, pl.ds(start, count, stride=stride), :] for b in range(ref.shape[0])], 1)


def store_rows(ref, start, stride, value):
    for b in range(ref.shape[0]):
        ref[b, pl.ds(start, value.shape[0], stride=stride), :] = value[:, 128 * b : 128 * b + 128]


def rows_by_y(source_ref, wide_ref, target_ref, ny):
    chans = source_ref.shape[0] // ny
    for b in range(wide_ref.shape[0]):
        wide_ref[b] = source_ref[:, 128 * b : 128 * b + 128].astype(F32)
    for y in range(ny):
        target_ref[y * chans : (y + 1) * chans, :] = load_rows(wide_ref, y, chans, ny).astype(BF16)


def fetches(cot_ref, side, plane_ref, sems):
    chunk = plane_ref.shape[0] // sems.shape[0]
    return [
        pltpu.make_async_copy(
            cot_ref.at[pl.ds(chunk * i, chunk), side], plane_ref.at[pl.ds(chunk * i, chunk)], sems.at[i]
        )
        for i in range(sems.shape[0])
    ]


def tap_rows(copies, plane_ref, even_ref, odd_ref, taps_ref):
    dout, ny2, nz2 = plane_ref.shape
    nz = nz2 // 2
    table = split_table()
    chunk = dout // len(copies)
    for i, copy in enumerate(copies):
        copy.wait()
        at = pl.ds(chunk * i * ny2, chunk * ny2)
        for b in range(nz2 // 256):
            block = plane_ref[chunk * i : chunk * i + chunk, :, 256 * b : 256 * b + 256]
            halves = dot(block.reshape(chunk * ny2, 256), table)
            even_ref[b, at, :] = halves[:, :128]
            odd_ref[b, at, :] = halves[:, 128:]

    def row(y, carry):
        even = load_rows(even_ref, y, dout, ny2)
        odd = load_rows(odd_ref, y, dout, ny2)
        base = pl.multiple_of((y + 1) * 4 * dout, 4 * dout)
        pieces = (pltpu.roll(odd, 1, 1), even, odd, pltpu.roll(even, nz - 1, 1))
        for k, piece in enumerate(pieces):
            taps_ref[pl.ds(base + k * dout, dout), :] = piece.astype(BF16)
        return carry

    lax.fori_loop(0, ny2, row, 0, unroll=4)
    group = 4 * dout
    taps_ref[:group, :] = taps_ref[ny2 * group : (ny2 + 1) * group, :]
    taps_ref[(ny2 + 1) * group :, :] = taps_ref[group : 2 * group, :]


def grad_weights(w_ref, own, nbr):
    both = jnp.concatenate([w_ref[own].astype(F32), w_ref[nbr].astype(F32)], 1)
    return both.T.astype(BF16)


def flatten(blocks_ref, out_ref):
    for b in range(blocks_ref.shape[0]):
        out_ref[:, 128 * b : 128 * b + 128] = blocks_ref[b]


def outer_kernel(
    core_ref, cot_ref, w_hbm_ref, taps_ref, vg_ref, partial_ref,
    plane_ref, even_ref, odd_ref, vg_blocks, partial_blocks, w_ref, sems, w_sem,
):
    dout, ny2, _ = plane_ref.shape
    ny, group, chans = ny2 // 2, 4 * dout, w_ref.shape[2]
    side, own, nbr = roles(core_ref[0])[1]
    copies = fetches(cot_ref, side, plane_ref, sems)
    w_copy = pltpu.make_async_copy(w_hbm_ref, w_ref, w_sem)
    for copy in copies + [w_copy]:
        copy.start()
    tap_rows(copies, plane_ref, even_ref, odd_ref, taps_ref)
    w_copy.wait()
    weights = grad_weights(w_ref, own, nbr)
    most = jnp.zeros((chans, vg_ref.shape[1]), F32)
    for y in range(ny):
        sums = dot(weights, taps_ref[y * 2 * group : (y * 2 + 4) * group, :])
        store_rows(vg_blocks, y, ny, sums[:chans])
        store_rows(partial_blocks, y, ny, sums[chans:])
        most = jnp.maximum(most, jnp.abs(sums[chans:]))
    flatten(vg_blocks, vg_ref)
    rows = chans * ny
    level = level_of(jnp.max(most, axis=0, keepdims=True))
    shrink = jnp.exp2(TOP - level)
    for b in range(partial_blocks.shape[0]):
        partial_ref[:rows, 128 * b : 128 * b + 128] = partial_blocks[b] * shrink
    partial_ref[rows:, :] = jnp.broadcast_to(level, (TAIL, partial_ref.shape[1]))


def tap_sums(taps_ref, own_t_ref, nbr_t_ref, sum_ref, before_ref):
    rows, chans = sum_ref.shape[0], sum_ref.shape[1] // 2
    for y in range(own_t_ref.shape[0] // chans):
        taps = taps_ref[y * rows // 2 : y * rows // 2 + rows, :]
        cells = jnp.concatenate([r[y * chans : (y + 1) * chans, :] for r in (own_t_ref, nbr_t_ref)], 0)
        grads = lax.dot_general(taps, cells, NT, preferred_element_type=F32)
        before = before_ref if y == 0 else sum_ref
        sum_ref[...] = grads if before is None else before[...] + grads


def inner_sums_kernel(
    core_ref, cot_ref, own_ref, inner_ref, taps_ref, own_t_ref, inner_t_ref, wg_ref,
    plane_ref, even_ref, odd_ref, wide_ref, sems,
):
    ny = plane_ref.shape[1] // 2
    copies = fetches(cot_ref, roles(core_ref[0])[0][0], plane_ref, sems)
    for copy in copies:
        copy.start()
    rows_by_y(own_ref, wide_ref, own_t_ref, ny)
    rows_by_y(inner_ref, wide_ref, inner_t_ref, ny)
    tap_rows(copies, plane_ref, even_ref, odd_ref, taps_ref)
    tap_sums(taps_ref, own_t_ref, inner_t_ref, wg_ref, None)


def inner_cells_kernel(core_ref, taps_ref, w_ref, vg_part_ref, vg_ref, partial_ref, vg_blocks, partial_blocks):
    chans, dout = w_ref.shape[2], w_ref.shape[1] // 16
    ny, group = vg_ref.shape[0] // chans, 4 * dout
    _, own, nbr = roles(core_ref[0])[0]
    weights = grad_weights(w_ref, own, nbr)
    for y in range(ny):
        sums = dot(weights, taps_ref[y * 2 * group : (y * 2 + 4) * group, :])
        store_rows(vg_blocks, y, ny, sums[:chans])
        store_rows(partial_blocks, y, ny, sums[chans:])
    for b in range(vg_blocks.shape[0]):
        at = slice(128 * b, 128 * b + 128)
        vg_ref[:, at] = vg_part_ref[:, at] + vg_blocks[b]
    flatten(partial_blocks, partial_ref)


def split(bit, whole_ref, keep_ref, send_ref):
    half = keep_ref.shape[0]
    keep_ref[...] = whole_ref[pl.ds(pl.multiple_of(bit * half, half), half), :]
    send_ref[...] = whole_ref[pl.ds(pl.multiple_of((1 - bit) * half, half), half), :]


def outer_sums_kernel(
    bits_ref, taps_ref, own_t_ref, outer_ref, arrived_ref, keep_ref, send_ref, outer_t_ref, wide_ref, sum_ref
):
    ny = outer_ref.shape[0] * 2 // arrived_ref.shape[1]
    rows_by_y(outer_ref, wide_ref, outer_t_ref, ny)
    tap_sums(taps_ref, own_t_ref, outer_t_ref, sum_ref, arrived_ref)
    split(bits_ref[1], sum_ref, keep_ref, send_ref)


def add_kernel(travelled, a_ref, b_ref, out_ref):
    shrink_into(grown(a_ref) + grown(b_ref) if travelled else a_ref[...] + b_ref[...], out_ref)


def join_kernel(bits_ref, mine_ref, there_ref, out_ref):
    bit, half = bits_ref[1], mine_ref.shape[0]
    out_ref[pl.ds(pl.multiple_of(bit * half, half), half), :] = mine_ref[...]
    out_ref[pl.ds(pl.multiple_of((1 - bit) * half, half), half), :] = there_ref[...]


def taps_kernel(scale, other, bits_ref, mine_ref, there_ref, *refs):
    out_ref, planes_ref, sems = refs[-3:]
    chans = out_ref.shape[2]
    core, bit = bits_ref[0], bits_ref[1]
    _, own, nbr = roles(1 - core if other else core)[1]
    for ref, place in ((mine_ref, bit), (there_ref, 1 - bit)):
        both = grown(ref) * scale
        half = both.shape[0]
        at = pl.ds(pl.multiple_of(place * half, half), half)
        planes_ref[0, at, :] = both[:, :chans]
        planes_ref[1, at, :] = both[:, chans:]
    copies = [
        pltpu.make_async_copy(planes_ref.at[i], out_ref.at[plane], sems.at[i]) for i, plane in enumerate((own, nbr))
    ]
    for copy in copies:
        copy.start()
    for copy in copies:
        copy.wait()


def cells_kernel(vg_ref, inner_ref, outer_ref, out_ref):
    out_ref[...] = (vg_ref[...] + inner_ref[...] + grown(outer_ref)).astype(BF16)


def fine_kernel(which, core_ref, own_t_ref, nbr_t_ref, w_ref, *refs):
    out_ref, plane_ref, even_ref, odd_ref, sem = refs[-5:]
    dout, ny2, nz2 = plane_ref.shape
    ny, nz = ny2 // 2, nz2 // 2
    chans = w_ref.shape[2]
    group = 4 * dout
    side, own, nbr = roles(core_ref[0])[which]
    for phase, step, taps in ((0, ny - 1, (1, 3)), (1, 1, (2, 0))):
        slabs = [w_ref[x, y * group : (y + 1) * group, :] for x in (own, nbr) for y in taps]
        weights = jnp.concatenate(slabs, 1)
        for y in range(ny):
            near = slice(y * chans, (y + 1) * chans)
            far = slice((y + step) % ny * chans, ((y + step) % ny + 1) * chans)
            cells = jnp.concatenate([r[at, :] for r in (own_t_ref, nbr_t_ref) for at in (near, far)], 0)
            sums = dot(weights, cells)
            even = sums[dout : 2 * dout] + pltpu.roll(sums[3 * dout :], 1, 1)
            odd = sums[2 * dout : 3 * dout] + pltpu.roll(sums[:dout], nz - 1, 1)
            store_rows(even_ref, 2 * y + phase, ny2, even)
            store_rows(odd_ref, 2 * y + phase, ny2, odd)
    table = join_table()
    for b in range(nz // 128):
        halves = jnp.concatenate([even_ref[b].astype(BF16), odd_ref[b].astype(BF16)], 1)
        fine = dot(halves, table).astype(BF16)
        plane_ref[:, :, 256 * b : 256 * b + 256] = fine.reshape(dout, ny2, 256)
    copy = pltpu.make_async_copy(plane_ref, out_ref.at[:, side], sem)
    copy.start()
    copy.wait()


VMEM = pl.BlockSpec(memory_space=pltpu.VMEM)
SMEM = pl.BlockSpec(memory_space=pltpu.SMEM)
HBM = pl.BlockSpec(memory_space=pltpu.HBM)


def call(kernel, in_specs, out_specs, outs, scratch, grant, flops=1_000, **more):
    return pl.pallas_call(
        kernel,
        out_shape=outs,
        in_specs=in_specs,
        out_specs=out_specs,
        scratch_shapes=scratch,
        compiler_params=pltpu.CompilerParams(vmem_limit_bytes=grant << 20),
        cost_estimate=pl.CostEstimate(flops=flops, bytes_accessed=1_000, transcendentals=0),
        **more,
    )


def together(*values):
    return lax.optimization_barrier(values)


def on_device(volume, weights, cotangent):
    chans, planes, ny, nz = volume.shape
    dout = cotangent.shape[0]
    peers = lax.axis_size("gx")
    me = lax.axis_index("gx")
    bits = jnp.stack([me & 1, (me >> 2) & 1, (me >> 1) & 1]).astype(jnp.int32)
    rows, wide, group = chans * ny, 16 * dout, 4 * dout
    struct = jax.ShapeDtypeStruct
    blocks_c, blocks_d = (nz // 128, rows, 128), (nz // 128, dout * 2 * ny, 128)
    taps_shape, plane_shape = ((2 * ny + 2) * group, nz), (dout, 2 * ny, 2 * nz)
    cells, wide_cells = struct((rows, nz), BF16), struct((rows, nz), F32)
    work = [pltpu.VMEM(plane_shape, BF16), pltpu.VMEM(blocks_d, F32), pltpu.VMEM(blocks_d, F32)]
    chunks = pltpu.SemaphoreType.DMA((4,))

    def swap(value, k):
        return lax.ppermute(value, "gx", [(i, i ^ k) for i in range(peers)])

    def beyond(value):
        return lax.ppermute(value, "gx", [(i, (i + (1 if i % 2 else -1)) % peers) for i in range(peers)])

    cotangent = pltpu.with_memory_space_constraint(cotangent, pltpu.HBM)
    own = volume.reshape(rows, nz)
    outer = beyond(own)
    inner = swap(own, 1)
    kernels = jnp.transpose(weights, (0, 1, 2, 4, 3)).reshape(4, wide, chans)

    taps_o, vg_o, to_outer = call(
        outer_kernel,
        [SMEM, HBM, HBM],
        [VMEM] * 3,
        [struct(taps_shape, BF16), wide_cells, struct((rows + TAIL, nz), F32)],
        work + [pltpu.VMEM(blocks_c, F32), pltpu.VMEM(blocks_c, F32), pltpu.VMEM(kernels.shape, BF16), chunks, pltpu.SemaphoreType.DMA],
        10,
        flops=COSTS[0],
    )(bits, cotangent, pltpu.with_memory_space_constraint(kernels, pltpu.HBM))
    to_outer = to_outer.astype(F16)
    own, vg_o = together(own, vg_o)

    taps_i, own_t, inner_t, wg_i = call(
        inner_sums_kernel,
        [SMEM, HBM, VMEM, VMEM],
        [VMEM] * 4,
        [struct(taps_shape, BF16), cells, cells, struct((wide, 2 * chans), F32)],
        work + [pltpu.VMEM(blocks_c, F32), chunks],
        8,
        flops=COSTS[1],
    )(bits, cotangent, own, inner)
    wg_arrived = swap(wg_i, 1)
    to_outer, taps_i = together(to_outer, taps_i)
    from_outer = beyond(to_outer)
    vg, to_inner = call(
        inner_cells_kernel,
        [SMEM, VMEM, VMEM, VMEM],
        [VMEM] * 2,
        [wide_cells, wide_cells],
        [pltpu.VMEM(blocks_c, F32), pltpu.VMEM(blocks_c, F32)],
        6,
        flops=COSTS[2],
    )(bits, taps_i, kernels, vg_o)

    def piece(n):
        return struct((wide // n, 2 * chans), F32)

    def fine(which, nbr_t, so_far):
        more = {} if so_far is None else {"input_output_aliases": {4: 0}}
        return call(
            functools.partial(fine_kernel, which),
            [SMEM, VMEM, VMEM, VMEM] + [HBM] * (so_far is not None),
            [HBM],
            [struct(cotangent.shape, BF16)],
            work + [pltpu.SemaphoreType.DMA],
            8,
            flops=COSTS[4],
            **more,
        )(bits, own_t, nbr_t, kernels, *([] if so_far is None else [so_far]))[0]

    own_t, vg = together(own_t, vg)
    keep, send, outer_t = call(
        outer_sums_kernel,
        [SMEM] + [VMEM] * 4,
        [VMEM] * 3,
        [piece(2), piece(2), cells],
        [pltpu.VMEM(blocks_c, F32), pltpu.VMEM((wide, 2 * chans), F32)],
        6,
        flops=COSTS[3],
    )(bits, taps_o, own_t, outer, wg_arrived)

    def add(travelled, a, b):
        rows = a.shape[0] + (0 if travelled else TAIL)
        kernel = functools.partial(add_kernel, travelled)
        return call(kernel, [VMEM] * 2, [VMEM], [struct((rows, a.shape[1]), F32)], [], 2)(a, b)[0].astype(F16)

    def cell_grads(from_inner, from_outer):
        return call(cells_kernel, [VMEM] * 3, [VMEM], [cells], [], 4)(vg, from_inner, from_outer)[0]

    send, inner_t = together(send, inner_t)
    upsampled = fine(0, inner_t, None)
    if peers & (peers - 1) or peers < 8:
        groups = [[i for i in range(peers) if i % 2 == c] for c in range(2)]
        total = call(join_kernel, [SMEM, VMEM, VMEM], [VMEM], [struct((wide, 2 * chans), F32)], [], 2)(bits, keep, send)
        total = lax.psum(total[0], "gx", axis_index_groups=groups).reshape(2, wide // 2, 2 * chans)
        mine, there = (lax.dynamic_index_in_dim(total, bit, 0, keepdims=False) for bit in (bits[1], 1 - bits[1]))
        mine, there = (add(False, x, jnp.zeros_like(x)) for x in (mine, there))
        other_mine = swap(mine, 1)
        upsampled = fine(1, outer_t, upsampled)
        volume_grad = cell_grads(swap(to_inner, 1), from_outer.astype(F32))
    else:
        mine = add(False, keep, swap(send, 4))
        mine, from_outer, to_inner, upsampled = together(mine, from_outer, to_inner, upsampled)
        from_inner = swap(to_inner, 1)
        mine = add(True, mine.astype(F32), swap(mine, 2).astype(F32))
        mine, outer_t, from_inner, from_outer = together(mine, outer_t, from_inner, from_outer)
        volume_grad = cell_grads(from_inner, from_outer.astype(F32))
        upsampled = fine(1, outer_t, upsampled)
        for k in range(3, peers.bit_length() - 1):
            mine = add(True, mine.astype(F32), swap(mine, 1 << k).astype(F32))
        mine, upsampled, volume_grad = together(mine, upsampled, volume_grad)
        there = swap(mine, 4)
        other_mine = swap(mine, 1)
    scale = 1.0 / math.sqrt(peers * planes * ny * nz)

    def taps(other, mine, there, so_far):
        more = {} if so_far is None else {"input_output_aliases": {3: 0}}
        return call(
            functools.partial(taps_kernel, scale, other),
            [SMEM, VMEM, VMEM] + [HBM] * (so_far is not None),
            [HBM],
            [struct((4, wide, chans), F32)],
            [pltpu.VMEM((2, wide, chans), F32), pltpu.SemaphoreType.DMA((2,))],
            4,
            **more,
        )(bits, mine.astype(F32), there.astype(F32), *([] if so_far is None else [so_far]))[0]

    other_there = swap(there, 1)
    weight_grad = taps(True, other_mine, other_there, taps(False, mine, there, None))
    weight_grad = jnp.transpose(weight_grad.reshape(4, 4, 4, dout, chans), (0, 1, 2, 4, 3))
    return (upsampled, volume_grad.reshape(volume.shape), weight_grad)


def solution(mesh):
    placed = (P(None, "gx", "groups", None), P(), P(None, "gx", "groups", None))
    return jax.shard_map(
        on_device,
        mesh=mesh,
        in_specs=placed,
        out_specs=(
            P(None, "gx", "groups", None),
            P(None, "gx", "groups", None),
            P("groups", None, None, None, None),
        ),
        check_vma=False,
    )
```

```python
import functools
import math

import jax
import jax.numpy as jnp
from jax import lax
from jax.experimental import pallas as pl
from jax.experimental.pallas import tpu as pltpu
from jax.sharding import PartitionSpec as P

F32 = jnp.float32
BF16 = jnp.bfloat16
F16 = jnp.float16
NT = (((1,), (1,)), ((), ()))
TOP = 14.0
TAIL = 16
COSTS = (1_000, 1_000, 1_000, 1_000, 1_000, 1_000, 12_000_000_000, 3_500_000_000)


def roles(core):
    inner = (1 - core, 2 - core, 3 * core)
    outer = (core, 1 + core, 3 - 3 * core)
    return inner, outer


def level_of(most):
    return jnp.ceil(jnp.log2(jnp.maximum(jnp.max(most, axis=1, keepdims=True), 1e-30)))


def shrink_into(value, out_ref):
    level = level_of(jnp.max(jnp.abs(value), axis=0, keepdims=True))
    out_ref[: value.shape[0], :] = value * jnp.exp2(TOP - level)
    out_ref[value.shape[0] :, :] = jnp.broadcast_to(level, (TAIL, value.shape[1]))


def grown(ref):
    rows = ref.shape[0] - TAIL
    return ref[:rows, :] * jnp.exp2(ref[rows : rows + 1, :] - TOP)


def dot(a, b):
    return jnp.dot(a, b, preferred_element_type=F32)


def split_table():
    row = lax.broadcasted_iota(jnp.int32, (256, 256), 0)
    col = lax.broadcasted_iota(jnp.int32, (256, 256), 1)
    return (row == jnp.where(col < 128, 2 * col, 2 * col - 255)).astype(BF16)


def join_table():
    row = lax.broadcasted_iota(jnp.int32, (256, 256), 0)
    col = lax.broadcasted_iota(jnp.int32, (256, 256), 1)
    return (col == jnp.where(row < 128, 2 * row, 2 * row - 255)).astype(BF16)


def load_rows(ref, start, count, stride):
    return jnp.concatenate([ref[b, pl.ds(start, count, stride=stride), :] for b in range(ref.shape[0])], 1)


def store_rows(ref, start, stride, value):
    for b in range(ref.shape[0]):
        ref[b, pl.ds(start, value.shape[0], stride=stride), :] = value[:, 128 * b : 128 * b + 128]


def rows_by_y(source_ref, wide_ref, target_ref, ny):
    chans = source_ref.shape[0] // ny
    for b in range(wide_ref.shape[0]):
        wide_ref[b] = source_ref[:, 128 * b : 128 * b + 128].astype(F32)
    for y in range(ny):
        target_ref[y * chans : (y + 1) * chans, :] = load_rows(wide_ref, y, chans, ny).astype(BF16)


def fetches(cot_ref, side, plane_ref, sems):
    chunk = plane_ref.shape[0] // sems.shape[0]
    return [
        pltpu.make_async_copy(
            cot_ref.at[pl.ds(chunk * i, chunk), side], plane_ref.at[pl.ds(chunk * i, chunk)], sems.at[i]
        )
        for i in range(sems.shape[0])
    ]


def tap_rows(copies, plane_ref, even_ref, odd_ref, taps_ref):
    dout, ny2, nz2 = plane_ref.shape
    nz = nz2 // 2
    table = split_table()
    chunk = dout // len(copies)
    for i, copy in enumerate(copies):
        copy.wait()
        at = pl.ds(chunk * i * ny2, chunk * ny2)
        for b in range(nz2 // 256):
            block = plane_ref[chunk * i : chunk * i + chunk, :, 256 * b : 256 * b + 256]
            halves = dot(block.reshape(chunk * ny2, 256), table)
            even_ref[b, at, :] = halves[:, :128]
            odd_ref[b, at, :] = halves[:, 128:]

    def row(y, carry):
        even = load_rows(even_ref, y, dout, ny2)
        odd = load_rows(odd_ref, y, dout, ny2)
        base = pl.multiple_of((y + 1) * 4 * dout, 4 * dout)
        pieces = (pltpu.roll(odd, 1, 1), even, odd, pltpu.roll(even, nz - 1, 1))
        for k, piece in enumerate(pieces):
            taps_ref[pl.ds(base + k * dout, dout), :] = piece.astype(BF16)
        return carry

    lax.fori_loop(0, ny2, row, 0, unroll=4)
    group = 4 * dout
    taps_ref[:group, :] = taps_ref[ny2 * group : (ny2 + 1) * group, :]
    taps_ref[(ny2 + 1) * group :, :] = taps_ref[group : 2 * group, :]


def grad_weights(w_ref, own, nbr):
    both = jnp.concatenate([w_ref[own].astype(F32), w_ref[nbr].astype(F32)], 1)
    return both.T.astype(BF16)


def flatten(blocks_ref, out_ref):
    for b in range(blocks_ref.shape[0]):
        out_ref[:, 128 * b : 128 * b + 128] = blocks_ref[b]


def outer_kernel(
    core_ref, cot_ref, w_hbm_ref, taps_ref, vg_ref, low_ref, high_ref,
    plane_ref, even_ref, odd_ref, vg_blocks, partial_blocks, w_ref, sems, w_sem,
):
    dout, ny2, _ = plane_ref.shape
    ny, group, chans = ny2 // 2, 4 * dout, w_ref.shape[2]
    side, own, nbr = roles(core_ref[0])[1]
    copies = fetches(cot_ref, side, plane_ref, sems)
    w_copy = pltpu.make_async_copy(w_hbm_ref, w_ref, w_sem)
    for copy in copies + [w_copy]:
        copy.start()
    tap_rows(copies, plane_ref, even_ref, odd_ref, taps_ref)
    w_copy.wait()
    weights = grad_weights(w_ref, own, nbr)
    most = jnp.zeros((chans, vg_ref.shape[1]), F32)
    for y in range(ny):
        sums = dot(weights, taps_ref[y * 2 * group : (y * 2 + 4) * group, :])
        store_rows(vg_blocks, y, ny, sums[:chans])
        store_rows(partial_blocks, y, ny, sums[chans:])
        most = jnp.maximum(most, jnp.abs(sums[chans:]))
    flatten(vg_blocks, vg_ref)
    level = level_of(jnp.max(most, axis=0, keepdims=True))
    shrink = jnp.exp2(TOP - level)
    start = 0
    for ref in (low_ref, high_ref):
        count = ref.shape[0] - TAIL
        for b in range(partial_blocks.shape[0]):
            ref[:count, 128 * b : 128 * b + 128] = partial_blocks[b, start : start + count, :] * shrink
        ref[count:, :] = jnp.broadcast_to(level, (TAIL, ref.shape[1]))
        start += count


def tap_sums(taps_ref, own_t_ref, nbr_t_ref, sum_ref, before_ref):
    rows, chans = sum_ref.shape[0], sum_ref.shape[1] // 2
    for y in range(own_t_ref.shape[0] // chans):
        taps = taps_ref[y * rows // 2 : y * rows // 2 + rows, :]
        cells = jnp.concatenate([r[y * chans : (y + 1) * chans, :] for r in (own_t_ref, nbr_t_ref)], 0)
        grads = lax.dot_general(taps, cells, NT, preferred_element_type=F32)
        before = before_ref if y == 0 else sum_ref
        sum_ref[...] = grads if before is None else before[...] + grads


def inner_sums_kernel(
    core_ref, cot_ref, own_ref, inner_ref, taps_ref, own_t_ref, inner_t_ref, wg_ref,
    plane_ref, even_ref, odd_ref, wide_ref, sems,
):
    ny = plane_ref.shape[1] // 2
    copies = fetches(cot_ref, roles(core_ref[0])[0][0], plane_ref, sems)
    for copy in copies:
        copy.start()
    rows_by_y(own_ref, wide_ref, own_t_ref, ny)
    rows_by_y(inner_ref, wide_ref, inner_t_ref, ny)
    tap_rows(copies, plane_ref, even_ref, odd_ref, taps_ref)
    tap_sums(taps_ref, own_t_ref, inner_t_ref, wg_ref, None)


def inner_cells_kernel(core_ref, taps_ref, w_ref, vg_part_ref, vg_ref, partial_ref, vg_blocks, partial_blocks):
    chans, dout = w_ref.shape[2], w_ref.shape[1] // 16
    ny, group = vg_ref.shape[0] // chans, 4 * dout
    _, own, nbr = roles(core_ref[0])[0]
    weights = grad_weights(w_ref, own, nbr)
    for y in range(ny):
        sums = dot(weights, taps_ref[y * 2 * group : (y * 2 + 4) * group, :])
        store_rows(vg_blocks, y, ny, sums[:chans])
        store_rows(partial_blocks, y, ny, sums[chans:])
    for b in range(vg_blocks.shape[0]):
        at = slice(128 * b, 128 * b + 128)
        vg_ref[:, at] = vg_part_ref[:, at] + vg_blocks[b]
    flatten(partial_blocks, partial_ref)


def outer_sums_kernel(taps_ref, own_t_ref, outer_ref, arrived_ref, send_ref, outer_t_ref, wide_ref, sum_ref):
    ny = outer_ref.shape[0] * 2 // arrived_ref.shape[1]
    rows_by_y(outer_ref, wide_ref, outer_t_ref, ny)
    tap_sums(taps_ref, own_t_ref, outer_t_ref, sum_ref, arrived_ref)
    shrink_into(sum_ref[...], send_ref)


def split_kernel(bits_ref, a_ref, b_ref, keep_ref, send_ref, sum_ref):
    bit, half = bits_ref[1], keep_ref.shape[0]
    sum_ref[...] = grown(a_ref) + grown(b_ref)
    keep_ref[...] = sum_ref[pl.ds(pl.multiple_of(bit * half, half), half), :]
    shrink_into(sum_ref[pl.ds(pl.multiple_of((1 - bit) * half, half), half), :], send_ref)


def add_kernel(travelled, a_ref, b_ref, out_ref):
    shrink_into((grown(a_ref) if travelled else a_ref[...]) + grown(b_ref), out_ref)


def taps_kernel(scale, bits_ref, mine_ref, there_ref, other_mine_ref, other_there_ref, out_ref, planes_ref, sems):
    chans = out_ref.shape[2]
    core, bit = bits_ref[0], bits_ref[1]
    copies = []
    for i, (side, refs) in enumerate(((core, (mine_ref, there_ref)), (1 - core, (other_mine_ref, other_there_ref)))):
        _, own, nbr = roles(side)[1]
        for ref, place in zip(refs, (bit, 1 - bit)):
            both = grown(ref) * scale
            half = both.shape[0]
            at = pl.ds(pl.multiple_of(place * half, half), half)
            planes_ref[2 * i, at, :] = both[:, :chans]
            planes_ref[2 * i + 1, at, :] = both[:, chans:]
        for j, plane in ((2 * i, own), (2 * i + 1, nbr)):
            copies.append(pltpu.make_async_copy(planes_ref.at[j], out_ref.at[plane], sems.at[j]))
            copies[-1].start()
    for copy in copies:
        copy.wait()


def cells_kernel(vg_ref, inner_ref, low_ref, high_ref, out_ref):
    count = low_ref.shape[0] - TAIL
    for at, ref in ((slice(0, count), low_ref), (slice(count, None), high_ref)):
        out_ref[at, :] = (vg_ref[at, :] + inner_ref[at, :] + grown(ref)).astype(BF16)


def fine_kernel(which, core_ref, own_t_ref, nbr_t_ref, w_ref, *refs):
    out_ref, plane_ref, even_ref, odd_ref, sem = refs[-5:]
    dout, ny2, nz2 = plane_ref.shape
    ny, nz = ny2 // 2, nz2 // 2
    chans = w_ref.shape[2]
    group = 4 * dout
    side, own, nbr = roles(core_ref[0])[which]
    for phase, step, taps in ((0, ny - 1, (1, 3)), (1, 1, (2, 0))):
        slabs = [w_ref[x, y * group : (y + 1) * group, :] for x in (own, nbr) for y in taps]
        weights = jnp.concatenate(slabs, 1)
        for y in range(ny):
            near = slice(y * chans, (y + 1) * chans)
            far = slice((y + step) % ny * chans, ((y + step) % ny + 1) * chans)
            cells = jnp.concatenate([r[at, :] for r in (own_t_ref, nbr_t_ref) for at in (near, far)], 0)
            sums = dot(weights, cells)
            even = sums[dout : 2 * dout] + pltpu.roll(sums[3 * dout :], 1, 1)
            odd = sums[2 * dout : 3 * dout] + pltpu.roll(sums[:dout], nz - 1, 1)
            store_rows(even_ref, 2 * y + phase, ny2, even)
            store_rows(odd_ref, 2 * y + phase, ny2, odd)
    table = join_table()
    chunk = dout // sem.shape[0]
    copies = []
    for i in range(sem.shape[0]):
        at = slice(chunk * i * ny2, chunk * (i + 1) * ny2)
        for b in range(nz // 128):
            halves = jnp.concatenate([even_ref[b, at, :].astype(BF16), odd_ref[b, at, :].astype(BF16)], 1)
            fine = dot(halves, table).astype(BF16)
            plane_ref[chunk * i : chunk * (i + 1), :, 256 * b : 256 * b + 256] = fine.reshape(chunk, ny2, 256)
        here = pl.ds(chunk * i, chunk)
        copies.append(pltpu.make_async_copy(plane_ref.at[here], out_ref.at[here, side], sem.at[i]))
        copies[-1].start()
    for copy in copies:
        copy.wait()


VMEM = pl.BlockSpec(memory_space=pltpu.VMEM)
SMEM = pl.BlockSpec(memory_space=pltpu.SMEM)
HBM = pl.BlockSpec(memory_space=pltpu.HBM)


def call(kernel, in_specs, out_specs, outs, scratch, grant, flops=1_000, **more):
    return pl.pallas_call(
        kernel,
        out_shape=outs,
        in_specs=in_specs,
        out_specs=out_specs,
        scratch_shapes=scratch,
        compiler_params=pltpu.CompilerParams(vmem_limit_bytes=grant << 20),
        cost_estimate=pl.CostEstimate(flops=flops, bytes_accessed=1_000, transcendentals=0),
        **more,
    )


def together(*values):
    return lax.optimization_barrier(values)


def on_device(volume, weights, cotangent):
    chans, planes, ny, nz = volume.shape
    dout = cotangent.shape[0]
    peers = lax.axis_size("gx")
    assert peers >= 16 and not peers & (peers - 1)
    me = lax.axis_index("gx")
    bits = jnp.stack([me & 1, (me >> 2) & 1, (me >> 1) & 1]).astype(jnp.int32)
    rows, wide, group = chans * ny, 16 * dout, 4 * dout
    struct = jax.ShapeDtypeStruct
    early = rows * 3 // 128 * 16
    blocks_c, blocks_d = (nz // 128, rows, 128), (nz // 128, dout * 2 * ny, 128)
    taps_shape, plane_shape = ((2 * ny + 2) * group, nz), (dout, 2 * ny, 2 * nz)
    cells, wide_cells = struct((rows, nz), BF16), struct((rows, nz), F32)
    work = [pltpu.VMEM(plane_shape, BF16), pltpu.VMEM(blocks_d, F32), pltpu.VMEM(blocks_d, F32)]
    chunks = pltpu.SemaphoreType.DMA((4,))

    def swap(value, k):
        return lax.ppermute(value, "gx", [(i, i ^ k) for i in range(peers)])

    def beyond(value):
        return lax.ppermute(value, "gx", [(i, (i + (1 if i % 2 else -1)) % peers) for i in range(peers)])

    cotangent = pltpu.with_memory_space_constraint(cotangent, pltpu.HBM)
    own = volume.reshape(rows, nz)
    outer = beyond(own)
    inner = swap(own, 1)
    kernels = jnp.transpose(weights, (0, 1, 2, 4, 3)).reshape(4, wide, chans)

    taps_o, vg_o, low, high = call(
        outer_kernel,
        [SMEM, HBM, HBM],
        [VMEM] * 4,
        [struct(taps_shape, BF16), wide_cells] + [struct((part + TAIL, nz), F32) for part in (early, rows - early)],
        work + [pltpu.VMEM(blocks_c, F32), pltpu.VMEM(blocks_c, F32), pltpu.VMEM(kernels.shape, BF16), chunks, pltpu.SemaphoreType.DMA],
        10,
        flops=COSTS[0],
    )(bits, cotangent, pltpu.with_memory_space_constraint(kernels, pltpu.HBM))
    low = low.astype(F16)
    own, vg_o = together(own, vg_o)

    taps_i, own_t, inner_t, wg_i = call(
        inner_sums_kernel,
        [SMEM, HBM, VMEM, VMEM],
        [VMEM] * 4,
        [struct(taps_shape, BF16), cells, cells, struct((wide, 2 * chans), F32)],
        work + [pltpu.VMEM(blocks_c, F32), chunks],
        8,
        flops=COSTS[1],
    )(bits, cotangent, own, inner)
    wg_arrived = swap(wg_i, 1)
    low, taps_i = together(low, taps_i)
    low = beyond(low)
    vg, to_inner = call(
        inner_cells_kernel,
        [SMEM, VMEM, VMEM, VMEM],
        [VMEM] * 2,
        [wide_cells, wide_cells],
        [pltpu.VMEM(blocks_c, F32), pltpu.VMEM(blocks_c, F32)],
        6,
        flops=COSTS[2],
    )(bits, taps_i, kernels, vg_o)

    def fine(which, nbr_t, so_far):
        more = {} if so_far is None else {"input_output_aliases": {4: 0}}
        return call(
            functools.partial(fine_kernel, which),
            [SMEM, VMEM, VMEM, VMEM] + [HBM] * (so_far is not None),
            [HBM],
            [struct(cotangent.shape, BF16)],
            work + [chunks],
            8,
            flops=COSTS[4 + which],
            **more,
        )(bits, own_t, nbr_t, kernels, *([] if so_far is None else [so_far]))[0]

    own_t, vg = together(own_t, vg)
    send, outer_t = call(
        outer_sums_kernel,
        [VMEM] * 4,
        [VMEM] * 2,
        [struct((wide + TAIL, 2 * chans), F32), cells],
        [pltpu.VMEM(blocks_c, F32), pltpu.VMEM((wide, 2 * chans), F32)],
        6,
        flops=COSTS[3],
    )(taps_o, own_t, outer, wg_arrived)
    send = send.astype(F16)

    def add(travelled, cost, a, b):
        rows = a.shape[0] + (0 if travelled else TAIL)
        kernel = functools.partial(add_kernel, travelled)
        return call(kernel, [VMEM] * 2, [VMEM], [struct((rows, a.shape[1]), F32)], [], 2, flops=cost)(a, b)[0].astype(F16)

    send, inner_t = together(send, inner_t)
    there = swap(send, 2)
    upsampled = fine(0, inner_t, None)
    there, upsampled = together(there, upsampled)
    keep, send = call(
        split_kernel,
        [SMEM, VMEM, VMEM],
        [VMEM] * 2,
        [struct((wide // 2, 2 * chans), F32), struct((wide // 2 + TAIL, 2 * chans), F32)],
        [pltpu.VMEM((wide, 2 * chans), F32)],
        2,
    )(bits, send.astype(F32), there.astype(F32))
    send = send.astype(F16)
    send, low, outer_t = together(send, low, outer_t)
    mine = add(False, COSTS[6], keep, swap(send, 4).astype(F32))
    mine, high, outer_t = together(mine, high.astype(F16), outer_t)
    there = swap(mine, 8)
    high = beyond(high)
    upsampled = fine(1, outer_t, upsampled)
    mine = add(True, COSTS[7], mine.astype(F32), there.astype(F32))
    for k in range(4, peers.bit_length() - 1):
        mine = add(True, COSTS[7], mine.astype(F32), swap(mine, 1 << k).astype(F32))
    mine, upsampled = together(mine, upsampled)
    from_inner = swap(to_inner, 1)
    there = swap(mine, 4)
    other_mine = swap(mine, 1)
    (volume_grad,) = call(cells_kernel, [VMEM] * 4, [VMEM], [cells], [], 4)(
        vg, from_inner, low.astype(F32), high.astype(F32)
    )
    there, volume_grad = together(there, volume_grad)
    other_there = swap(there, 1)
    scale = 1.0 / math.sqrt(peers * planes * ny * nz)
    (weight_grad,) = call(
        functools.partial(taps_kernel, scale),
        [SMEM] + [VMEM] * 4,
        [HBM],
        [struct((4, wide, chans), F32)],
        [pltpu.VMEM((4, wide, chans), F32), pltpu.SemaphoreType.DMA((4,))],
        4,
    )(bits, *(value.astype(F32) for value in (mine, there, other_mine, other_there)))
    weight_grad = jnp.transpose(weight_grad.reshape(4, 4, 4, dout, chans), (0, 1, 2, 4, 3))
    return (upsampled, volume_grad.reshape(volume.shape), weight_grad)


def solution(mesh):
    placed = (P(None, "gx", "groups", None), P(), P(None, "gx", "groups", None))
    return jax.shard_map(
        on_device,
        mesh=mesh,
        in_specs=placed,
        out_specs=(
            P(None, "gx", "groups", None),
            P(None, "gx", "groups", None),
            P("groups", None, None, None, None),
        ),
        check_vma=False,
    )
```

```python
import functools
import math

import jax
import jax.numpy as jnp
from jax import lax
from jax.experimental import pallas as pl
from jax.experimental.pallas import tpu as pltpu
from jax.sharding import PartitionSpec as P

F32 = jnp.float32
BF16 = jnp.bfloat16
F16 = jnp.float16
NT = (((1,), (1,)), ((), ()))
TOP = 14.0
TAIL = 16
COSTS = (1_000, 1_000, 1_000, 1_000, 1_000, 1_000, 8_000_000_000, 2_000_000_000, 1_000)


def roles(core):
    inner = (1 - core, 2 - core, 3 * core)
    outer = (core, 1 + core, 3 - 3 * core)
    return inner, outer


def level_of(most):
    return jnp.ceil(jnp.log2(jnp.maximum(jnp.max(most, axis=1, keepdims=True), 1e-30)))


def shrink_into(value, out_ref):
    level = level_of(jnp.max(jnp.abs(value), axis=0, keepdims=True))
    out_ref[: value.shape[0], :] = value * jnp.exp2(TOP - level)
    out_ref[value.shape[0] :, :] = jnp.broadcast_to(level, (TAIL, value.shape[1]))


def grown(ref):
    rows = ref.shape[0] - TAIL
    return ref[:rows, :] * jnp.exp2(ref[rows : rows + 1, :] - TOP)


def dot(a, b):
    return jnp.dot(a, b, preferred_element_type=F32)


def split_table():
    row = lax.broadcasted_iota(jnp.int32, (256, 256), 0)
    col = lax.broadcasted_iota(jnp.int32, (256, 256), 1)
    return (row == jnp.where(col < 128, 2 * col, 2 * col - 255)).astype(BF16)


def join_table():
    row = lax.broadcasted_iota(jnp.int32, (256, 256), 0)
    col = lax.broadcasted_iota(jnp.int32, (256, 256), 1)
    return (col == jnp.where(row < 128, 2 * row, 2 * row - 255)).astype(BF16)


def load_rows(ref, start, count, stride):
    return jnp.concatenate([ref[b, pl.ds(start, count, stride=stride), :] for b in range(ref.shape[0])], 1)


def store_rows(ref, start, stride, value):
    for b in range(ref.shape[0]):
        ref[b, pl.ds(start, value.shape[0], stride=stride), :] = value[:, 128 * b : 128 * b + 128]


def rows_by_y(source_ref, wide_ref, target_ref, ny):
    chans = source_ref.shape[0] // ny
    for b in range(wide_ref.shape[0]):
        wide_ref[b] = source_ref[:, 128 * b : 128 * b + 128].astype(F32)
    for y in range(ny):
        target_ref[y * chans : (y + 1) * chans, :] = load_rows(wide_ref, y, chans, ny).astype(BF16)


def tap_rows(cot_ref, side, even_ref, odd_ref, taps_ref, copies=(None,)):
    dout, _, ny2, nz2 = cot_ref.shape
    nz = nz2 // 2
    table = split_table()
    chunk = dout // len(copies)
    for i, copy in enumerate(copies):
        if copy is not None:
            copy.wait()
        at = slice(chunk * i * ny2, chunk * (i + 1) * ny2)
        for b in range(nz2 // 256):
            block = cot_ref[chunk * i : chunk * (i + 1), side, :, 256 * b : 256 * b + 256]
            halves = dot(block.reshape(chunk * ny2, 256), table)
            even_ref[b, at, :] = halves[:, :128]
            odd_ref[b, at, :] = halves[:, 128:]

    def row(y, carry):
        even = load_rows(even_ref, y, dout, ny2)
        odd = load_rows(odd_ref, y, dout, ny2)
        base = pl.multiple_of((y + 1) * 4 * dout, 4 * dout)
        pieces = (pltpu.roll(odd, 1, 1), even, odd, pltpu.roll(even, nz - 1, 1))
        for k, piece in enumerate(pieces):
            taps_ref[pl.ds(base + k * dout, dout), :] = piece.astype(BF16)
        return carry

    lax.fori_loop(0, ny2, row, 0, unroll=True)
    group = 4 * dout
    taps_ref[:group, :] = taps_ref[ny2 * group : (ny2 + 1) * group, :]
    taps_ref[(ny2 + 1) * group :, :] = taps_ref[group : 2 * group, :]


def grad_weights(w_ref, own, nbr):
    both = jnp.concatenate([w_ref[own].astype(F32), w_ref[nbr].astype(F32)], 1)
    return both.T.astype(BF16)


def flatten(blocks_ref, out_ref):
    for b in range(blocks_ref.shape[0]):
        out_ref[:, 128 * b : 128 * b + 128] = blocks_ref[b]


def outer_kernel(
    core_ref, cot_ref, w_hbm_ref, taps_ref, vg_ref, low_ref, high_ref,
    plane_ref, even_ref, odd_ref, vg_blocks, partial_blocks, w_ref, sems,
):
    dout, _, ny2, _ = cot_ref.shape
    ny, group, chans = ny2 // 2, 4 * dout, w_ref.shape[2]
    side, own, nbr = roles(core_ref[0])[1]
    chunk = dout // 4
    copies = [
        pltpu.make_async_copy(
            cot_ref.at[pl.ds(chunk * i, chunk), pl.ds(side, 1)], plane_ref.at[pl.ds(chunk * i, chunk)], sems.at[i]
        )
        for i in range(4)
    ] + [pltpu.make_async_copy(w_hbm_ref, w_ref, sems.at[4])]
    for copy in copies:
        copy.start()
    tap_rows(plane_ref, 0, even_ref, odd_ref, taps_ref, copies[:4])
    copies[4].wait()
    weights = grad_weights(w_ref, own, nbr)
    most = jnp.zeros((chans, vg_ref.shape[1]), F32)
    for y in range(ny):
        sums = dot(weights, taps_ref[y * 2 * group : (y * 2 + 4) * group, :])
        store_rows(vg_blocks, y, ny, sums[:chans])
        store_rows(partial_blocks, y, ny, sums[chans:])
        most = jnp.maximum(most, jnp.abs(sums[chans:]))
    flatten(vg_blocks, vg_ref)
    level = level_of(jnp.max(most, axis=0, keepdims=True))
    shrink = jnp.exp2(TOP - level)
    start = 0
    for ref in (low_ref, high_ref):
        count = ref.shape[0] - TAIL
        for b in range(partial_blocks.shape[0]):
            ref[:count, 128 * b : 128 * b + 128] = partial_blocks[b, start : start + count, :] * shrink
        ref[count:, :] = jnp.broadcast_to(level, (TAIL, ref.shape[1]))
        start += count


def tap_sums(taps_ref, own_t_ref, nbr_t_ref, sum_ref, before_ref):
    rows, chans = sum_ref.shape[0], sum_ref.shape[1] // 2
    for y in range(own_t_ref.shape[0] // chans):
        taps = taps_ref[y * rows // 2 : y * rows // 2 + rows, :]
        cells = jnp.concatenate([r[y * chans : (y + 1) * chans, :] for r in (own_t_ref, nbr_t_ref)], 0)
        grads = lax.dot_general(taps, cells, NT, preferred_element_type=F32)
        before = before_ref if y == 0 else sum_ref
        sum_ref[...] = grads if before is None else before[...] + grads


def inner_sums_kernel(
    core_ref, cot_ref, own_ref, inner_ref, taps_ref, own_t_ref, inner_t_ref, wg_ref, even_ref, odd_ref, wide_ref
):
    ny = cot_ref.shape[2] // 2
    rows_by_y(own_ref, wide_ref, own_t_ref, ny)
    rows_by_y(inner_ref, wide_ref, inner_t_ref, ny)
    tap_rows(cot_ref, roles(core_ref[0])[0][0], even_ref, odd_ref, taps_ref)
    tap_sums(taps_ref, own_t_ref, inner_t_ref, wg_ref, None)


def inner_cells_kernel(core_ref, taps_ref, w_ref, vg_part_ref, vg_ref, partial_ref, vg_blocks, partial_blocks):
    chans, dout = w_ref.shape[2], w_ref.shape[1] // 16
    ny, group = vg_ref.shape[0] // chans, 4 * dout
    _, own, nbr = roles(core_ref[0])[0]
    weights = grad_weights(w_ref, own, nbr)
    for y in range(ny):
        sums = dot(weights, taps_ref[y * 2 * group : (y * 2 + 4) * group, :])
        store_rows(vg_blocks, y, ny, sums[:chans])
        store_rows(partial_blocks, y, ny, sums[chans:])
    for b in range(vg_blocks.shape[0]):
        at = slice(128 * b, 128 * b + 128)
        vg_ref[:, at] = vg_part_ref[:, at] + vg_blocks[b]
    flatten(partial_blocks, partial_ref)


def outer_sums_kernel(taps_ref, own_t_ref, outer_ref, arrived_ref, send_ref, outer_t_ref, wide_ref, sum_ref):
    ny = outer_ref.shape[0] * 2 // arrived_ref.shape[1]
    rows_by_y(outer_ref, wide_ref, outer_t_ref, ny)
    tap_sums(taps_ref, own_t_ref, outer_t_ref, sum_ref, arrived_ref)
    shrink_into(sum_ref[...], send_ref)


def add_kernel(a_ref, b_ref, out_ref):
    shrink_into(grown(a_ref) + grown(b_ref), out_ref)


def taps_kernel(scale, bits_ref, mine_ref, other_ref, out_ref, planes_ref, sems):
    chans = out_ref.shape[2]
    core = bits_ref[0]
    copies = []
    for i, (side, ref) in enumerate(((core, mine_ref), (1 - core, other_ref))):
        _, own, nbr = roles(side)[1]
        both = grown(ref) * scale
        for j, plane, part in ((2 * i, own, both[:, :chans]), (2 * i + 1, nbr, both[:, chans:])):
            planes_ref[j] = part
            copies.append(pltpu.make_async_copy(planes_ref.at[j], out_ref.at[plane], sems.at[j]))
            copies[-1].start()
    for copy in copies:
        copy.wait()


def cells_kernel(vg_ref, inner_ref, low_ref, high_ref, out_ref):
    count = low_ref.shape[0] - TAIL
    for at, ref in ((slice(0, count), low_ref), (slice(count, None), high_ref)):
        out_ref[at, :] = (vg_ref[at, :] + inner_ref[at, :] + grown(ref)).astype(BF16)


def fine_kernel(which, core_ref, own_t_ref, nbr_t_ref, w_ref, *refs):
    out_ref, plane_ref, even_ref, odd_ref, sem = refs[-5:]
    dout, ny2, nz2 = plane_ref.shape
    ny, nz = ny2 // 2, nz2 // 2
    chans = w_ref.shape[2]
    group = 4 * dout
    side, own, nbr = roles(core_ref[0])[which]
    for phase, step, taps in ((0, ny - 1, (1, 3)), (1, 1, (2, 0))):
        slabs = [w_ref[x, y * group : (y + 1) * group, :] for x in (own, nbr) for y in taps]
        weights = jnp.concatenate(slabs, 1)
        for y in range(ny):
            near = slice(y * chans, (y + 1) * chans)
            far = slice((y + step) % ny * chans, ((y + step) % ny + 1) * chans)
            cells = jnp.concatenate([r[at, :] for r in (own_t_ref, nbr_t_ref) for at in (near, far)], 0)
            sums = dot(weights, cells)
            even = sums[dout : 2 * dout] + pltpu.roll(sums[3 * dout :], 1, 1)
            odd = sums[2 * dout : 3 * dout] + pltpu.roll(sums[:dout], nz - 1, 1)
            store_rows(even_ref, 2 * y + phase, ny2, even)
            store_rows(odd_ref, 2 * y + phase, ny2, odd)
    table = join_table()
    chunk = dout // sem.shape[0]
    copies = []
    for i in range(sem.shape[0]):
        at = slice(chunk * i * ny2, chunk * (i + 1) * ny2)
        for b in range(nz // 128):
            halves = jnp.concatenate([even_ref[b, at, :].astype(BF16), odd_ref[b, at, :].astype(BF16)], 1)
            fine = dot(halves, table).astype(BF16)
            plane_ref[chunk * i : chunk * (i + 1), :, 256 * b : 256 * b + 256] = fine.reshape(chunk, ny2, 256)
        here = pl.ds(chunk * i, chunk)
        copies.append(pltpu.make_async_copy(plane_ref.at[here], out_ref.at[here, side], sem.at[i]))
        copies[-1].start()
    for copy in copies:
        copy.wait()


VMEM = pl.BlockSpec(memory_space=pltpu.VMEM)
SMEM = pl.BlockSpec(memory_space=pltpu.SMEM)
HBM = pl.BlockSpec(memory_space=pltpu.HBM)


def call(kernel, in_specs, out_specs, outs, scratch, grant, flops=1_000, **more):
    return pl.pallas_call(
        kernel,
        out_shape=outs,
        in_specs=in_specs,
        out_specs=out_specs,
        scratch_shapes=scratch,
        compiler_params=pltpu.CompilerParams(vmem_limit_bytes=grant << 20),
        cost_estimate=pl.CostEstimate(flops=flops, bytes_accessed=1_000, transcendentals=0),
        **more,
    )


def together(*values):
    return lax.optimization_barrier(values)


def on_device(volume, weights, cotangent):
    chans, planes, ny, nz = volume.shape
    dout = cotangent.shape[0]
    peers = lax.axis_size("gx")
    assert peers >= 16 and not peers & (peers - 1)
    me = lax.axis_index("gx")
    bits = (me & 1).astype(jnp.int32).reshape(1)
    rows, wide, group = chans * ny, 16 * dout, 4 * dout
    struct = jax.ShapeDtypeStruct
    early = rows // 512 * 16 * 12
    blocks_c, blocks_d = (nz // 128, rows, 128), (nz // 128, dout * 2 * ny, 128)
    taps_shape, plane_shape = ((2 * ny + 2) * group, nz), (dout, 2 * ny, 2 * nz)
    cells, wide_cells = struct((rows, nz), BF16), struct((rows, nz), F32)
    work = [pltpu.VMEM(plane_shape, BF16), pltpu.VMEM(blocks_d, F32), pltpu.VMEM(blocks_d, F32)]
    chunks = pltpu.SemaphoreType.DMA((4,))

    def swap(value, k):
        return lax.ppermute(value, "gx", [(i, i ^ k) for i in range(peers)])

    def beyond(value):
        return lax.ppermute(value, "gx", [(i, (i + (1 if i % 2 else -1)) % peers) for i in range(peers)])

    own = volume.reshape(rows, nz)
    outer = beyond(own)
    inner = swap(own, 1)
    kernels = jnp.transpose(weights, (0, 1, 2, 4, 3)).reshape(4, wide, chans)

    taps_o, vg_o, low, high = call(
        outer_kernel,
        [SMEM, HBM, HBM],
        [VMEM] * 4,
        [struct(taps_shape, BF16), wide_cells] + [struct((part + TAIL, nz), F32) for part in (early, rows - early)],
        [pltpu.VMEM((dout, 1, 2 * ny, 2 * nz), BF16)] + work[1:]
        + [pltpu.VMEM(blocks_c, F32), pltpu.VMEM(blocks_c, F32), pltpu.VMEM(kernels.shape, BF16), pltpu.SemaphoreType.DMA((5,))],
        10,
        flops=COSTS[0],
    )(bits, *(pltpu.with_memory_space_constraint(value, pltpu.HBM) for value in (cotangent, kernels)))
    low = low.astype(F16)
    own, vg_o = together(own, vg_o)

    taps_i, own_t, inner_t, wg_i = call(
        inner_sums_kernel,
        [SMEM, VMEM, VMEM, VMEM],
        [VMEM] * 4,
        [struct(taps_shape, BF16), cells, cells, struct((wide, 2 * chans), F32)],
        work[1:] + [pltpu.VMEM(blocks_c, F32)],
        6,
        flops=COSTS[1],
    )(bits, cotangent, own, inner)
    wg_arrived = swap(wg_i, 1)
    low, taps_i = together(low, taps_i)
    low = beyond(low)
    vg, to_inner = call(
        inner_cells_kernel,
        [SMEM, VMEM, VMEM, VMEM],
        [VMEM] * 2,
        [wide_cells, wide_cells],
        [pltpu.VMEM(blocks_c, F32), pltpu.VMEM(blocks_c, F32)],
        6,
        flops=COSTS[2],
    )(bits, taps_i, kernels, vg_o)

    def fine(which, nbr_t, so_far):
        more = {} if so_far is None else {"input_output_aliases": {4: 0}}
        return call(
            functools.partial(fine_kernel, which),
            [SMEM, VMEM, VMEM, VMEM] + [HBM] * (so_far is not None),
            [HBM],
            [struct(cotangent.shape, BF16)],
            work + [chunks],
            8,
            flops=COSTS[4 + which],
            **more,
        )(bits, own_t, nbr_t, kernels, *([] if so_far is None else [so_far]))[0]

    own_t, vg = together(own_t, vg)
    send, outer_t = call(
        outer_sums_kernel,
        [VMEM] * 4,
        [VMEM] * 2,
        [struct((wide + TAIL, 2 * chans), F32), cells],
        [pltpu.VMEM(blocks_c, F32), pltpu.VMEM((wide, 2 * chans), F32)],
        6,
        flops=COSTS[3],
    )(taps_o, own_t, outer, wg_arrived)
    send = send.astype(F16)

    def add(cost, a, b):
        out = struct(a.shape, F32)
        return call(add_kernel, [VMEM] * 2, [VMEM], [out], [], 2, flops=cost)(a.astype(F32), b.astype(F32))[0].astype(F16)

    mine, inner_t = together(send, inner_t)
    there = swap(mine, 2)
    upsampled = fine(0, inner_t, None)
    there, upsampled = together(there, upsampled)
    mine = add(COSTS[8], mine, there)
    mine, low, outer_t = together(mine, low, outer_t)
    from_inner = swap(to_inner, 1)
    mine = add(COSTS[6], mine, swap(mine, 4))
    mine, high, outer_t = together(mine, high.astype(F16), outer_t)
    there = swap(mine, 8)
    high = beyond(high)
    upsampled = fine(1, outer_t, upsampled)
    there, upsampled = together(there, upsampled)
    mine = add(COSTS[7], mine, there)
    for k in range(4, peers.bit_length() - 1):
        mine = add(COSTS[7], mine, swap(mine, 1 << k))
    other = swap(mine, 1)
    scale = 1.0 / math.sqrt(peers * planes * ny * nz)
    (weight_grad,) = call(
        functools.partial(taps_kernel, scale),
        [SMEM] + [VMEM] * 2,
        [HBM],
        [struct((4, wide, chans), F32)],
        [pltpu.VMEM((4, wide, chans), F32), pltpu.SemaphoreType.DMA((4,))],
        4,
    )(bits, mine.astype(F32), other.astype(F32))
    high, weight_grad = together(high, weight_grad)
    (volume_grad,) = call(cells_kernel, [VMEM] * 4, [VMEM], [cells], [], 4)(
        vg, from_inner, low.astype(F32), high.astype(F32)
    )
    weight_grad = jnp.transpose(weight_grad.reshape(4, 4, 4, dout, chans), (0, 1, 2, 4, 3))
    return (upsampled, volume_grad.reshape(volume.shape), weight_grad)


def solution(mesh):
    placed = (P(None, "gx", "groups", None), P(), P(None, "gx", "groups", None))
    return jax.shard_map(
        on_device,
        mesh=mesh,
        in_specs=placed,
        out_specs=(
            P(None, "gx", "groups", None),
            P(None, "gx", "groups", None),
            P("groups", None, None, None, None),
        ),
        check_vma=False,
    )
```

```python
import functools
import math

import jax
import jax.numpy as jnp
from jax import lax
from jax.experimental import pallas as pl
from jax.experimental.pallas import tpu as pltpu
from jax.sharding import PartitionSpec as P

F32 = jnp.float32
BF16 = jnp.bfloat16
F16 = jnp.float16
NT = (((1,), (1,)), ((), ()))
TOP = 14.0
TAIL = 16
COSTS = (1_000, 1_000, 1_000, 1_000, 1_000, 1_000, 1_000, 1_000, 8_000_000_000)


def roles(core):
    inner = (1 - core, 2 - core, 3 * core)
    outer = (core, 1 + core, 3 - 3 * core)
    return inner, outer


def level_of(most):
    return jnp.ceil(jnp.log2(jnp.maximum(jnp.max(most, axis=1, keepdims=True), 1e-30)))


def shrink_into(value, out_ref):
    level = level_of(jnp.max(jnp.abs(value), axis=0, keepdims=True))
    out_ref[: value.shape[0], :] = value * jnp.exp2(TOP - level)
    out_ref[value.shape[0] :, :] = jnp.broadcast_to(level, (TAIL, value.shape[1]))


def grown(ref):
    rows = ref.shape[0] - TAIL
    return ref[:rows, :] * jnp.exp2(ref[rows : rows + 1, :] - TOP)


def dot(a, b):
    return jnp.dot(a, b, preferred_element_type=F32)


def split_table():
    row = lax.broadcasted_iota(jnp.int32, (256, 256), 0)
    col = lax.broadcasted_iota(jnp.int32, (256, 256), 1)
    return (row == jnp.where(col < 128, 2 * col, 2 * col - 255)).astype(BF16)


def join_table():
    row = lax.broadcasted_iota(jnp.int32, (256, 256), 0)
    col = lax.broadcasted_iota(jnp.int32, (256, 256), 1)
    return (col == jnp.where(row < 128, 2 * row, 2 * row - 255)).astype(BF16)


def load_rows(ref, start, count, stride):
    return jnp.concatenate([ref[b, pl.ds(start, count, stride=stride), :] for b in range(ref.shape[0])], 1)


def store_rows(ref, start, stride, value):
    for b in range(ref.shape[0]):
        ref[b, pl.ds(start, value.shape[0], stride=stride), :] = value[:, 128 * b : 128 * b + 128]


def rows_by_y(source_ref, wide_ref, target_ref, ny):
    chans = source_ref.shape[0] // ny
    for b in range(wide_ref.shape[0]):
        wide_ref[b] = source_ref[:, 128 * b : 128 * b + 128].astype(F32)
    for y in range(ny):
        target_ref[y * chans : (y + 1) * chans, :] = load_rows(wide_ref, y, chans, ny).astype(BF16)


def tap_rows(cot_ref, side, even_ref, odd_ref, taps_ref, copies=(None,)):
    dout, _, ny2, nz2 = cot_ref.shape
    nz = nz2 // 2
    table = split_table()
    chunk = dout // len(copies)
    for i, copy in enumerate(copies):
        if copy is not None:
            copy.wait()
        at = slice(chunk * i * ny2, chunk * (i + 1) * ny2)
        for b in range(nz2 // 256):
            block = cot_ref[chunk * i : chunk * (i + 1), side, :, 256 * b : 256 * b + 256]
            halves = dot(block.reshape(chunk * ny2, 256), table)
            even_ref[b, at, :] = halves[:, :128]
            odd_ref[b, at, :] = halves[:, 128:]

    def row(y, carry):
        even = load_rows(even_ref, y, dout, ny2)
        odd = load_rows(odd_ref, y, dout, ny2)
        base = pl.multiple_of((y + 1) * 4 * dout, 4 * dout)
        pieces = (pltpu.roll(odd, 1, 1), even, odd, pltpu.roll(even, nz - 1, 1))
        for k, piece in enumerate(pieces):
            taps_ref[pl.ds(base + k * dout, dout), :] = piece.astype(BF16)
        return carry

    lax.fori_loop(0, ny2, row, 0, unroll=True)
    group = 4 * dout
    taps_ref[:group, :] = taps_ref[ny2 * group : (ny2 + 1) * group, :]
    taps_ref[(ny2 + 1) * group :, :] = taps_ref[group : 2 * group, :]


def grad_weights(w_ref, own, nbr):
    both = jnp.concatenate([w_ref[own].astype(F32), w_ref[nbr].astype(F32)], 1)
    return both.T.astype(BF16)


def flatten(blocks_ref, out_ref):
    for b in range(blocks_ref.shape[0]):
        out_ref[:, 128 * b : 128 * b + 128] = blocks_ref[b]


def outer_kernel(
    core_ref, cot_ref, w_hbm_ref, taps_ref, vg_ref, partial_ref,
    plane_ref, even_ref, odd_ref, vg_blocks, partial_blocks, w_ref, sems,
):
    dout, _, ny2, _ = cot_ref.shape
    ny, group, chans = ny2 // 2, 4 * dout, w_ref.shape[2]
    side, own, nbr = roles(core_ref[0])[1]
    chunk = dout // 4
    copies = [
        pltpu.make_async_copy(
            cot_ref.at[pl.ds(chunk * i, chunk), pl.ds(side, 1)], plane_ref.at[pl.ds(chunk * i, chunk)], sems.at[i]
        )
        for i in range(4)
    ] + [pltpu.make_async_copy(w_hbm_ref, w_ref, sems.at[4])]
    for copy in copies:
        copy.start()
    tap_rows(plane_ref, 0, even_ref, odd_ref, taps_ref, copies[:4])
    copies[4].wait()
    weights = grad_weights(w_ref, own, nbr)
    most = jnp.zeros((chans, vg_ref.shape[1]), F32)
    for y in range(ny):
        sums = dot(weights, taps_ref[y * 2 * group : (y * 2 + 4) * group, :])
        store_rows(vg_blocks, y, ny, sums[:chans])
        store_rows(partial_blocks, y, ny, sums[chans:])
        most = jnp.maximum(most, jnp.abs(sums[chans:]))
    flatten(vg_blocks, vg_ref)
    level = level_of(jnp.max(most, axis=0, keepdims=True))
    shrink = jnp.exp2(TOP - level)
    rows = chans * ny
    for b in range(partial_blocks.shape[0]):
        partial_ref[:rows, 128 * b : 128 * b + 128] = partial_blocks[b] * shrink
    partial_ref[rows:, :] = jnp.broadcast_to(level, (TAIL, partial_ref.shape[1]))


def tap_sums(taps_ref, own_t_ref, nbr_t_ref, sum_ref, before_ref):
    rows, chans = sum_ref.shape[0], sum_ref.shape[1] // 2
    for y in range(own_t_ref.shape[0] // chans):
        taps = taps_ref[y * rows // 2 : y * rows // 2 + rows, :]
        cells = jnp.concatenate([r[y * chans : (y + 1) * chans, :] for r in (own_t_ref, nbr_t_ref)], 0)
        grads = lax.dot_general(taps, cells, NT, preferred_element_type=F32)
        before = before_ref if y == 0 else sum_ref
        sum_ref[...] = grads if before is None else before[...] + grads


def inner_sums_kernel(
    core_ref, cot_ref, own_ref, inner_ref, taps_ref, own_t_ref, inner_t_ref, wg_ref, even_ref, odd_ref, wide_ref
):
    ny = cot_ref.shape[2] // 2
    rows_by_y(own_ref, wide_ref, own_t_ref, ny)
    rows_by_y(inner_ref, wide_ref, inner_t_ref, ny)
    tap_rows(cot_ref, roles(core_ref[0])[0][0], even_ref, odd_ref, taps_ref)
    tap_sums(taps_ref, own_t_ref, inner_t_ref, wg_ref, None)


def inner_cells_kernel(core_ref, taps_ref, w_ref, vg_part_ref, vg_ref, partial_ref, vg_blocks, partial_blocks):
    chans, dout = w_ref.shape[2], w_ref.shape[1] // 16
    ny, group = vg_ref.shape[0] // chans, 4 * dout
    _, own, nbr = roles(core_ref[0])[0]
    weights = grad_weights(w_ref, own, nbr)
    for y in range(ny):
        sums = dot(weights, taps_ref[y * 2 * group : (y * 2 + 4) * group, :])
        store_rows(vg_blocks, y, ny, sums[:chans])
        store_rows(partial_blocks, y, ny, sums[chans:])
    for b in range(vg_blocks.shape[0]):
        at = slice(128 * b, 128 * b + 128)
        vg_ref[:, at] = vg_part_ref[:, at] + vg_blocks[b]
    flatten(partial_blocks, partial_ref)


def outer_sums_kernel(taps_ref, own_t_ref, outer_ref, arrived_ref, send_ref, outer_t_ref, wide_ref, sum_ref):
    ny = outer_ref.shape[0] * 2 // arrived_ref.shape[1]
    rows_by_y(outer_ref, wide_ref, outer_t_ref, ny)
    tap_sums(taps_ref, own_t_ref, outer_t_ref, sum_ref, arrived_ref)
    shrink_into(sum_ref[...], send_ref)


def add_kernel(a_ref, b_ref, out_ref):
    shrink_into(grown(a_ref) + grown(b_ref), out_ref)


def taps_kernel(scale, bits_ref, mine_ref, other_ref, out_ref, planes_ref, sems):
    chans = out_ref.shape[2]
    core = bits_ref[0]
    copies = []
    for i, (side, ref) in enumerate(((core, mine_ref), (1 - core, other_ref))):
        _, own, nbr = roles(side)[1]
        both = grown(ref) * scale
        for j, plane, part in ((2 * i, own, both[:, :chans]), (2 * i + 1, nbr, both[:, chans:])):
            planes_ref[j] = part
            copies.append(pltpu.make_async_copy(planes_ref.at[j], out_ref.at[plane], sems.at[j]))
            copies[-1].start()
    for copy in copies:
        copy.wait()


def cells_kernel(vg_ref, inner_ref, outer_ref, out_ref):
    out_ref[...] = (vg_ref[...] + inner_ref[...] + grown(outer_ref)).astype(BF16)


def fine_kernel(which, core_ref, own_t_ref, nbr_t_ref, w_ref, *refs):
    out_ref, plane_ref, even_ref, odd_ref, sem = refs[-5:]
    dout, ny2, nz2 = plane_ref.shape
    ny, nz = ny2 // 2, nz2 // 2
    chans = w_ref.shape[2]
    group = 4 * dout
    side, own, nbr = roles(core_ref[0])[which]
    for phase, step, taps in ((0, ny - 1, (1, 3)), (1, 1, (2, 0))):
        slabs = [w_ref[x, y * group : (y + 1) * group, :] for x in (own, nbr) for y in taps]
        weights = jnp.concatenate(slabs, 1)
        for y in range(ny):
            near = slice(y * chans, (y + 1) * chans)
            far = slice((y + step) % ny * chans, ((y + step) % ny + 1) * chans)
            cells = jnp.concatenate([r[at, :] for r in (own_t_ref, nbr_t_ref) for at in (near, far)], 0)
            sums = dot(weights, cells)
            even = sums[dout : 2 * dout] + pltpu.roll(sums[3 * dout :], 1, 1)
            odd = sums[2 * dout : 3 * dout] + pltpu.roll(sums[:dout], nz - 1, 1)
            store_rows(even_ref, 2 * y + phase, ny2, even)
            store_rows(odd_ref, 2 * y + phase, ny2, odd)
    table = join_table()
    chunk = dout // sem.shape[0]
    copies = []
    for i in range(sem.shape[0]):
        at = slice(chunk * i * ny2, chunk * (i + 1) * ny2)
        for b in range(nz // 128):
            halves = jnp.concatenate([even_ref[b, at, :].astype(BF16), odd_ref[b, at, :].astype(BF16)], 1)
            fine = dot(halves, table).astype(BF16)
            plane_ref[chunk * i : chunk * (i + 1), :, 256 * b : 256 * b + 256] = fine.reshape(chunk, ny2, 256)
        here = pl.ds(chunk * i, chunk)
        copies.append(pltpu.make_async_copy(plane_ref.at[here], out_ref.at[here, side], sem.at[i]))
        copies[-1].start()
    for copy in copies:
        copy.wait()


VMEM = pl.BlockSpec(memory_space=pltpu.VMEM)
SMEM = pl.BlockSpec(memory_space=pltpu.SMEM)
HBM = pl.BlockSpec(memory_space=pltpu.HBM)


def call(kernel, in_specs, out_specs, outs, scratch, grant, flops=1_000, **more):
    return pl.pallas_call(
        kernel,
        out_shape=outs,
        in_specs=in_specs,
        out_specs=out_specs,
        scratch_shapes=scratch,
        compiler_params=pltpu.CompilerParams(vmem_limit_bytes=grant << 20),
        cost_estimate=pl.CostEstimate(flops=flops, bytes_accessed=1_000, transcendentals=0),
        **more,
    )


def together(*values):
    return lax.optimization_barrier(values)


def on_device(volume, weights, cotangent):
    chans, planes, ny, nz = volume.shape
    dout = cotangent.shape[0]
    peers = lax.axis_size("gx")
    assert peers >= 16 and not peers & (peers - 1)
    me = lax.axis_index("gx")
    bits = (me & 1).astype(jnp.int32).reshape(1)
    rows, wide, group = chans * ny, 16 * dout, 4 * dout
    struct = jax.ShapeDtypeStruct
    blocks_c, blocks_d = (nz // 128, rows, 128), (nz // 128, dout * 2 * ny, 128)
    taps_shape, plane_shape = ((2 * ny + 2) * group, nz), (dout, 2 * ny, 2 * nz)
    cells, wide_cells = struct((rows, nz), BF16), struct((rows, nz), F32)
    work = [pltpu.VMEM(plane_shape, BF16), pltpu.VMEM(blocks_d, F32), pltpu.VMEM(blocks_d, F32)]
    chunks = pltpu.SemaphoreType.DMA((4,))

    def swap(value, k):
        return lax.ppermute(value, "gx", [(i, i ^ k) for i in range(peers)])

    def beyond(value):
        return lax.ppermute(value, "gx", [(i, (i + (1 if i % 2 else -1)) % peers) for i in range(peers)])

    own = volume.reshape(rows, nz)
    outer = beyond(own)
    inner = swap(own, 1)
    kernels = jnp.transpose(weights, (0, 1, 2, 4, 3)).reshape(4, wide, chans)

    taps_o, vg_o, low = call(
        outer_kernel,
        [SMEM, HBM, HBM],
        [VMEM] * 3,
        [struct(taps_shape, BF16), wide_cells] + [struct((rows + TAIL, nz), F32)],
        [pltpu.VMEM((dout, 1, 2 * ny, 2 * nz), BF16)] + work[1:]
        + [pltpu.VMEM(blocks_c, F32), pltpu.VMEM(blocks_c, F32), pltpu.VMEM(kernels.shape, BF16), pltpu.SemaphoreType.DMA((5,))],
        10,
        flops=COSTS[0],
    )(bits, *(pltpu.with_memory_space_constraint(value, pltpu.HBM) for value in (cotangent, kernels)))
    low = low.astype(F16)
    own, vg_o = together(own, vg_o)

    taps_i, own_t, inner_t, wg_i = call(
        inner_sums_kernel,
        [SMEM, VMEM, VMEM, VMEM],
        [VMEM] * 4,
        [struct(taps_shape, BF16), cells, cells, struct((wide, 2 * chans), F32)],
        work[1:] + [pltpu.VMEM(blocks_c, F32)],
        6,
        flops=COSTS[1],
    )(bits, cotangent, own, inner)
    wg_arrived = swap(wg_i, 1)
    low, taps_i = together(low, taps_i)
    low = beyond(low)
    vg, to_inner = call(
        inner_cells_kernel,
        [SMEM, VMEM, VMEM, VMEM],
        [VMEM] * 2,
        [wide_cells, wide_cells],
        [pltpu.VMEM(blocks_c, F32), pltpu.VMEM(blocks_c, F32)],
        6,
        flops=COSTS[2],
    )(bits, taps_i, kernels, vg_o)

    def fine(which, nbr_t, so_far):
        more = {} if so_far is None else {"input_output_aliases": {4: 0}}
        return call(
            functools.partial(fine_kernel, which),
            [SMEM, VMEM, VMEM, VMEM] + [HBM] * (so_far is not None),
            [HBM],
            [struct(cotangent.shape, BF16)],
            work + [chunks],
            8,
            flops=COSTS[4 + which],
            **more,
        )(bits, own_t, nbr_t, kernels, *([] if so_far is None else [so_far]))[0]

    own_t, vg = together(own_t, vg)
    send, outer_t = call(
        outer_sums_kernel,
        [VMEM] * 4,
        [VMEM] * 2,
        [struct((wide + TAIL, 2 * chans), F32), cells],
        [pltpu.VMEM(blocks_c, F32), pltpu.VMEM((wide, 2 * chans), F32)],
        6,
        flops=COSTS[3],
    )(taps_o, own_t, outer, wg_arrived)
    send = send.astype(F16)

    def add(cost, a, b):
        out = struct(a.shape, F32)
        return call(add_kernel, [VMEM] * 2, [VMEM], [out], [], 2, flops=cost)(a.astype(F32), b.astype(F32))[0].astype(F16)

    mine, inner_t = together(send, inner_t)
    there = swap(mine, 4)
    upsampled = fine(0, inner_t, None)
    there, upsampled = together(there, upsampled)
    mine = add(COSTS[6], mine, there)
    mine, low, outer_t = together(mine, low, outer_t)
    from_inner = swap(to_inner, 1)
    mine = add(COSTS[8], mine, swap(mine, 2))
    mine, outer_t, low, from_inner = together(mine, outer_t, low, from_inner)
    there = swap(mine, 8)
    upsampled = fine(1, outer_t, upsampled)
    (volume_grad,) = call(cells_kernel, [VMEM] * 3, [VMEM], [cells], [], 4)(vg, from_inner, low.astype(F32))
    there, upsampled, volume_grad = together(there, upsampled, volume_grad)
    mine = add(COSTS[7], mine, there)
    for k in range(4, peers.bit_length() - 1):
        mine = add(COSTS[7], mine, swap(mine, 1 << k))
    other = swap(mine, 1)
    scale = 1.0 / math.sqrt(peers * planes * ny * nz)
    (weight_grad,) = call(
        functools.partial(taps_kernel, scale),
        [SMEM] + [VMEM] * 2,
        [HBM],
        [struct((4, wide, chans), F32)],
        [pltpu.VMEM((4, wide, chans), F32), pltpu.SemaphoreType.DMA((4,))],
        4,
    )(bits, mine.astype(F32), other.astype(F32))
    weight_grad = jnp.transpose(weight_grad.reshape(4, 4, 4, dout, chans), (0, 1, 2, 4, 3))
    return (upsampled, volume_grad.reshape(volume.shape), weight_grad)


def solution(mesh):
    placed = (P(None, "gx", "groups", None), P(), P(None, "gx", "groups", None))
    return jax.shard_map(
        on_device,
        mesh=mesh,
        in_specs=placed,
        out_specs=(
            P(None, "gx", "groups", None),
            P(None, "gx", "groups", None),
            P("groups", None, None, None, None),
        ),
        check_vma=False,
    )
```

```python
import functools
import math

import jax
import jax.numpy as jnp
from jax import lax
from jax.experimental import pallas as pl
from jax.experimental.pallas import tpu as pltpu
from jax.sharding import PartitionSpec as P

F32 = jnp.float32
BF16 = jnp.bfloat16
F16 = jnp.float16
NT = (((1,), (1,)), ((), ()))
TOP = 14.0
TAIL = 16
COSTS = (1_000, 1_000, 1_000, 1_000, 1_000, 1_000, 1_000, 1_000, 8_000_000_000)


def roles(core):
    inner = (1 - core, 2 - core, 3 * core)
    outer = (core, 1 + core, 3 - 3 * core)
    return inner, outer


def level_of(most):
    return jnp.ceil(jnp.log2(jnp.maximum(jnp.max(most, axis=1, keepdims=True), 1e-30)))


def shrink_into(value, out_ref):
    level = level_of(jnp.max(jnp.abs(value), axis=0, keepdims=True))
    out_ref[: value.shape[0], :] = value * jnp.exp2(TOP - level)
    out_ref[value.shape[0] :, :] = jnp.broadcast_to(level, (TAIL, value.shape[1]))


def grown(ref):
    rows = ref.shape[0] - TAIL
    return ref[:rows, :] * jnp.exp2(ref[rows : rows + 1, :] - TOP)


def dot(a, b):
    return jnp.dot(a, b, preferred_element_type=F32)


def split_table():
    row = lax.broadcasted_iota(jnp.int32, (256, 256), 0)
    col = lax.broadcasted_iota(jnp.int32, (256, 256), 1)
    return (row == jnp.where(col < 128, 2 * col, 2 * col - 255)).astype(BF16)


def join_table():
    row = lax.broadcasted_iota(jnp.int32, (256, 256), 0)
    col = lax.broadcasted_iota(jnp.int32, (256, 256), 1)
    return (col == jnp.where(row < 128, 2 * row, 2 * row - 255)).astype(BF16)


def load_rows(ref, start, count, stride):
    return jnp.concatenate([ref[b, pl.ds(start, count, stride=stride), :] for b in range(ref.shape[0])], 1)


def store_rows(ref, start, stride, value):
    for b in range(ref.shape[0]):
        ref[b, pl.ds(start, value.shape[0], stride=stride), :] = value[:, 128 * b : 128 * b + 128]


def rows_by_y(source_ref, wide_ref, target_ref, ny):
    chans = source_ref.shape[0] // ny
    for b in range(wide_ref.shape[0]):
        wide_ref[b] = source_ref[:, 128 * b : 128 * b + 128].astype(F32)
    for y in range(ny):
        target_ref[y * chans : (y + 1) * chans, :] = load_rows(wide_ref, y, chans, ny).astype(BF16)


def tap_rows(cot_ref, side, even_ref, odd_ref, taps_ref, copies=(None,)):
    dout, _, ny2, nz2 = cot_ref.shape
    nz = nz2 // 2
    table = split_table()
    chunk = dout // len(copies)
    for i, copy in enumerate(copies):
        if copy is not None:
            copy.wait()
        at = slice(chunk * i * ny2, chunk * (i + 1) * ny2)
        for b in range(nz2 // 256):
            block = cot_ref[chunk * i : chunk * (i + 1), side, :, 256 * b : 256 * b + 256]
            halves = dot(block.reshape(chunk * ny2, 256), table)
            even_ref[b, at, :] = halves[:, :128]
            odd_ref[b, at, :] = halves[:, 128:]

    def row(y, carry):
        even = load_rows(even_ref, y, dout, ny2)
        odd = load_rows(odd_ref, y, dout, ny2)
        base = pl.multiple_of((y + 1) * 4 * dout, 4 * dout)
        pieces = (pltpu.roll(odd, 1, 1), even, odd, pltpu.roll(even, nz - 1, 1))
        for k, piece in enumerate(pieces):
            taps_ref[pl.ds(base + k * dout, dout), :] = piece.astype(BF16)
        return carry

    lax.fori_loop(0, ny2, row, 0, unroll=True)
    group = 4 * dout
    taps_ref[:group, :] = taps_ref[ny2 * group : (ny2 + 1) * group, :]
    taps_ref[(ny2 + 1) * group :, :] = taps_ref[group : 2 * group, :]


def grad_weights(w_ref, own, nbr):
    both = jnp.concatenate([w_ref[own].astype(F32), w_ref[nbr].astype(F32)], 1)
    return both.T.astype(BF16)


def flatten(blocks_ref, out_ref):
    for b in range(blocks_ref.shape[0]):
        out_ref[:, 128 * b : 128 * b + 128] = blocks_ref[b]


def outer_kernel(
    core_ref, cot_ref, w_hbm_ref, taps_ref, vg_ref, partial_ref,
    plane_ref, even_ref, odd_ref, vg_blocks, partial_blocks, w_ref, sems,
):
    dout, _, ny2, _ = cot_ref.shape
    ny, group, chans = ny2 // 2, 4 * dout, w_ref.shape[2]
    side, own, nbr = roles(core_ref[0])[1]
    chunk = dout // 4
    copies = [
        pltpu.make_async_copy(
            cot_ref.at[pl.ds(chunk * i, chunk), pl.ds(side, 1)], plane_ref.at[pl.ds(chunk * i, chunk)], sems.at[i]
        )
        for i in range(4)
    ] + [pltpu.make_async_copy(w_hbm_ref, w_ref, sems.at[4])]
    for copy in copies:
        copy.start()
    tap_rows(plane_ref, 0, even_ref, odd_ref, taps_ref, copies[:4])
    copies[4].wait()
    weights = grad_weights(w_ref, own, nbr)
    most = jnp.zeros((chans, vg_ref.shape[1]), F32)
    for y in range(ny):
        sums = dot(weights, taps_ref[y * 2 * group : (y * 2 + 4) * group, :])
        store_rows(vg_blocks, y, ny, sums[:chans])
        store_rows(partial_blocks, y, ny, sums[chans:])
        most = jnp.maximum(most, jnp.abs(sums[chans:]))
    flatten(vg_blocks, vg_ref)
    level = level_of(jnp.max(most, axis=0, keepdims=True))
    shrink = jnp.exp2(TOP - level)
    rows = chans * ny
    for b in range(partial_blocks.shape[0]):
        partial_ref[:rows, 128 * b : 128 * b + 128] = partial_blocks[b] * shrink
    partial_ref[rows:, :] = jnp.broadcast_to(level, (TAIL, partial_ref.shape[1]))


def tap_sums(taps_ref, own_t_ref, nbr_t_ref, sum_ref, before_ref):
    rows, chans = sum_ref.shape[0], sum_ref.shape[1] // 2
    for y in range(own_t_ref.shape[0] // chans):
        taps = taps_ref[y * rows // 2 : y * rows // 2 + rows, :]
        cells = jnp.concatenate([r[y * chans : (y + 1) * chans, :] for r in (own_t_ref, nbr_t_ref)], 0)
        grads = lax.dot_general(taps, cells, NT, preferred_element_type=F32)
        before = before_ref if y == 0 else sum_ref
        sum_ref[...] = grads if before is None else before[...] + grads


def inner_sums_kernel(
    core_ref, cot_ref, own_ref, inner_ref, taps_ref, own_t_ref, inner_t_ref, wg_ref, even_ref, odd_ref, wide_ref
):
    ny = cot_ref.shape[2] // 2
    rows_by_y(own_ref, wide_ref, own_t_ref, ny)
    rows_by_y(inner_ref, wide_ref, inner_t_ref, ny)
    tap_rows(cot_ref, roles(core_ref[0])[0][0], even_ref, odd_ref, taps_ref)
    tap_sums(taps_ref, own_t_ref, inner_t_ref, wg_ref, None)


def inner_cells_kernel(core_ref, taps_ref, w_ref, vg_part_ref, vg_ref, partial_ref, vg_blocks, partial_blocks):
    chans, dout = w_ref.shape[2], w_ref.shape[1] // 16
    ny, group = vg_ref.shape[0] // chans, 4 * dout
    _, own, nbr = roles(core_ref[0])[0]
    weights = grad_weights(w_ref, own, nbr)
    for y in range(ny):
        sums = dot(weights, taps_ref[y * 2 * group : (y * 2 + 4) * group, :])
        store_rows(vg_blocks, y, ny, sums[:chans])
        store_rows(partial_blocks, y, ny, sums[chans:])
    for b in range(vg_blocks.shape[0]):
        at = slice(128 * b, 128 * b + 128)
        vg_ref[:, at] = vg_part_ref[:, at] + vg_blocks[b]
    flatten(partial_blocks, partial_ref)


def outer_sums_kernel(taps_ref, own_t_ref, outer_ref, arrived_ref, send_ref, outer_t_ref, wide_ref, sum_ref):
    ny = outer_ref.shape[0] * 2 // arrived_ref.shape[1]
    rows_by_y(outer_ref, wide_ref, outer_t_ref, ny)
    tap_sums(taps_ref, own_t_ref, outer_t_ref, sum_ref, arrived_ref)
    shrink_into(sum_ref[...], send_ref)


def add_kernel(a_ref, b_ref, out_ref):
    shrink_into(grown(a_ref) + grown(b_ref), out_ref)


def taps_kernel(scale, bits_ref, mine_ref, other_ref, out_ref, planes_ref, sems):
    chans = out_ref.shape[2]
    core = bits_ref[0]
    copies = []
    for i, (side, ref) in enumerate(((core, mine_ref), (1 - core, other_ref))):
        _, own, nbr = roles(side)[1]
        both = grown(ref) * scale
        for j, plane, part in ((2 * i, own, both[:, :chans]), (2 * i + 1, nbr, both[:, chans:])):
            planes_ref[j] = part
            copies.append(pltpu.make_async_copy(planes_ref.at[j], out_ref.at[plane], sems.at[j]))
            copies[-1].start()
    for copy in copies:
        copy.wait()


def cells_kernel(vg_ref, inner_ref, outer_ref, out_ref):
    out_ref[...] = (vg_ref[...] + inner_ref[...] + grown(outer_ref)).astype(BF16)


def fine_kernel(which, core_ref, own_t_ref, nbr_t_ref, w_ref, *refs):
    out_ref, plane_ref, even_ref, odd_ref, sem = refs[-5:]
    dout, ny2, nz2 = plane_ref.shape
    ny, nz = ny2 // 2, nz2 // 2
    chans = w_ref.shape[2]
    group = 4 * dout
    side, own, nbr = roles(core_ref[0])[which]
    for phase, step, taps in ((0, ny - 1, (1, 3)), (1, 1, (2, 0))):
        slabs = [w_ref[x, y * group : (y + 1) * group, :] for x in (own, nbr) for y in taps]
        weights = jnp.concatenate(slabs, 1)
        for y in range(ny):
            near = slice(y * chans, (y + 1) * chans)
            far = slice((y + step) % ny * chans, ((y + step) % ny + 1) * chans)
            cells = jnp.concatenate([r[at, :] for r in (own_t_ref, nbr_t_ref) for at in (near, far)], 0)
            sums = dot(weights, cells)
            even = sums[dout : 2 * dout] + pltpu.roll(sums[3 * dout :], 1, 1)
            odd = sums[2 * dout : 3 * dout] + pltpu.roll(sums[:dout], nz - 1, 1)
            store_rows(even_ref, 2 * y + phase, ny2, even)
            store_rows(odd_ref, 2 * y + phase, ny2, odd)
    table = join_table()
    chunk = dout // sem.shape[0]
    copies = []
    for i in range(sem.shape[0]):
        at = slice(chunk * i * ny2, chunk * (i + 1) * ny2)
        for b in range(nz // 128):
            halves = jnp.concatenate([even_ref[b, at, :].astype(BF16), odd_ref[b, at, :].astype(BF16)], 1)
            fine = dot(halves, table).astype(BF16)
            plane_ref[chunk * i : chunk * (i + 1), :, 256 * b : 256 * b + 256] = fine.reshape(chunk, ny2, 256)
        here = pl.ds(chunk * i, chunk)
        copies.append(pltpu.make_async_copy(plane_ref.at[here], out_ref.at[here, side], sem.at[i]))
        copies[-1].start()
    for copy in copies:
        copy.wait()


VMEM = pl.BlockSpec(memory_space=pltpu.VMEM)
SMEM = pl.BlockSpec(memory_space=pltpu.SMEM)
HBM = pl.BlockSpec(memory_space=pltpu.HBM)


def call(kernel, in_specs, out_specs, outs, scratch, grant, flops=1_000, **more):
    return pl.pallas_call(
        kernel,
        out_shape=outs,
        in_specs=in_specs,
        out_specs=out_specs,
        scratch_shapes=scratch,
        compiler_params=pltpu.CompilerParams(vmem_limit_bytes=grant << 20),
        cost_estimate=pl.CostEstimate(flops=flops, bytes_accessed=1_000, transcendentals=0),
        **more,
    )


def together(*values):
    return lax.optimization_barrier(values)


def on_device(volume, weights, cotangent):
    chans, planes, ny, nz = volume.shape
    dout = cotangent.shape[0]
    peers = lax.axis_size("gx")
    assert peers >= 16 and not peers & (peers - 1)
    me = lax.axis_index("gx")
    bits = (me & 1).astype(jnp.int32).reshape(1)
    rows, wide, group = chans * ny, 16 * dout, 4 * dout
    struct = jax.ShapeDtypeStruct
    blocks_c, blocks_d = (nz // 128, rows, 128), (nz // 128, dout * 2 * ny, 128)
    taps_shape, plane_shape = ((2 * ny + 2) * group, nz), (dout, 2 * ny, 2 * nz)
    cells, wide_cells = struct((rows, nz), BF16), struct((rows, nz), F32)
    work = [pltpu.VMEM(plane_shape, BF16), pltpu.VMEM(blocks_d, F32), pltpu.VMEM(blocks_d, F32)]
    chunks = pltpu.SemaphoreType.DMA((4,))

    def swap(value, k):
        return lax.ppermute(value, "gx", [(i, i ^ k) for i in range(peers)])

    def beyond(value):
        return lax.ppermute(value, "gx", [(i, (i + (1 if i % 2 else -1)) % peers) for i in range(peers)])

    own = volume.reshape(rows, nz)
    outer = beyond(own)
    inner = swap(own, 1)
    kernels = jnp.transpose(weights, (0, 1, 2, 4, 3)).reshape(4, wide, chans)

    taps_o, vg_o, low = call(
        outer_kernel,
        [SMEM, HBM, HBM],
        [VMEM] * 3,
        [struct(taps_shape, BF16), wide_cells] + [struct((rows + TAIL, nz), F32)],
        [pltpu.VMEM((dout, 1, 2 * ny, 2 * nz), BF16)] + work[1:]
        + [pltpu.VMEM(blocks_c, F32), pltpu.VMEM(blocks_c, F32), pltpu.VMEM(kernels.shape, BF16), pltpu.SemaphoreType.DMA((5,))],
        10,
        flops=COSTS[0],
    )(bits, *(pltpu.with_memory_space_constraint(value, pltpu.HBM) for value in (cotangent, kernels)))
    low = low.astype(F16)
    own, vg_o = together(own, vg_o)

    taps_i, own_t, inner_t, wg_i = call(
        inner_sums_kernel,
        [SMEM, VMEM, VMEM, VMEM],
        [VMEM] * 4,
        [struct(taps_shape, BF16), cells, cells, struct((wide, 2 * chans), F32)],
        work[1:] + [pltpu.VMEM(blocks_c, F32)],
        6,
        flops=COSTS[1],
    )(bits, cotangent, own, inner)
    wg_arrived = swap(wg_i, 1)
    low, taps_i = together(low, taps_i)
    low = beyond(low)
    vg, to_inner = call(
        inner_cells_kernel,
        [SMEM, VMEM, VMEM, VMEM],
        [VMEM] * 2,
        [wide_cells, wide_cells],
        [pltpu.VMEM(blocks_c, F32), pltpu.VMEM(blocks_c, F32)],
        6,
        flops=COSTS[2],
    )(bits, taps_i, kernels, vg_o)

    def fine(which, nbr_t, so_far):
        more = {} if so_far is None else {"input_output_aliases": {4: 0}}
        return call(
            functools.partial(fine_kernel, which),
            [SMEM, VMEM, VMEM, VMEM] + [HBM] * (so_far is not None),
            [HBM],
            [struct(cotangent.shape, BF16)],
            work + [chunks],
            8,
            flops=COSTS[4 + which],
            **more,
        )(bits, own_t, nbr_t, kernels, *([] if so_far is None else [so_far]))[0]

    own_t, vg = together(own_t, vg)
    send, outer_t = call(
        outer_sums_kernel,
        [VMEM] * 4,
        [VMEM] * 2,
        [struct((wide + TAIL, 2 * chans), F32), cells],
        [pltpu.VMEM(blocks_c, F32), pltpu.VMEM((wide, 2 * chans), F32)],
        6,
        flops=COSTS[3],
    )(taps_o, own_t, outer, wg_arrived)
    send = send.astype(F16)

    def add(cost, a, b):
        out = struct(a.shape, F32)
        return call(add_kernel, [VMEM] * 2, [VMEM], [out], [], 2, flops=cost)(a.astype(F32), b.astype(F32))[0].astype(F16)

    mine, inner_t = together(send, inner_t)
    there = swap(mine, 4)
    upsampled = fine(0, inner_t, None)
    there, upsampled = together(there, upsampled)
    mine = add(COSTS[6], mine, there)
    mine, low, outer_t = together(mine, low, outer_t)
    from_inner = swap(to_inner, 1)
    there = swap(mine, 8)
    upsampled = fine(1, outer_t, upsampled)
    there, upsampled = together(there, upsampled)
    mine = add(COSTS[8], mine, there)
    mine, low, from_inner = together(mine, low, from_inner)
    there = swap(mine, 2)
    (volume_grad,) = call(cells_kernel, [VMEM] * 3, [VMEM], [cells], [], 4)(vg, from_inner, low.astype(F32))
    there, volume_grad = together(there, volume_grad)
    mine = add(COSTS[7], mine, there)
    for k in range(4, peers.bit_length() - 1):
        mine = add(COSTS[7], mine, swap(mine, 1 << k))
    other = swap(mine, 1)
    scale = 1.0 / math.sqrt(peers * planes * ny * nz)
    (weight_grad,) = call(
        functools.partial(taps_kernel, scale),
        [SMEM] + [VMEM] * 2,
        [HBM],
        [struct((4, wide, chans), F32)],
        [pltpu.VMEM((4, wide, chans), F32), pltpu.SemaphoreType.DMA((4,))],
        4,
    )(bits, mine.astype(F32), other.astype(F32))
    weight_grad = jnp.transpose(weight_grad.reshape(4, 4, 4, dout, chans), (0, 1, 2, 4, 3))
    return (upsampled, volume_grad.reshape(volume.shape), weight_grad)


def solution(mesh):
    placed = (P(None, "gx", "groups", None), P(), P(None, "gx", "groups", None))
    return jax.shard_map(
        on_device,
        mesh=mesh,
        in_specs=placed,
        out_specs=(
            P(None, "gx", "groups", None),
            P(None, "gx", "groups", None),
            P("groups", None, None, None, None),
        ),
        check_vma=False,
    )
```
